256 devices in a mesh: dp: 4 (over x), ctx: 64 (over y, z, core).
Axes of the slice: x: 4, y: 4, z: 8, core: 2. Of those that a mesh axis runs over, the one named last changes fastest.
Arguments:
- doc_start: int32 [4, 64], P('dp'), may hold values from 0 to 8191, as said below
- doc_end: int32 [4, 64], P('dp'), may hold values from 1 to 8192, as said below
- modality: int32 [4, 64], P('dp'), may hold values from 0 to 1
- x_in: bfloat16 [4, 8192, 4096], P('dp', 'ctx'), may hold values from -5 to 5
- log_decay: float32 [4, 64, 8192], P('dp', None, 'ctx'), may hold values from -1 to 0, as said below
- b_in: bfloat16 [4, 8192, 512], P('dp', 'ctx'), may hold values from -2.5 to 2.5
- c_in: bfloat16 [4, 8192, 512], P('dp', 'ctx'), may hold values from -2.5 to 2.5
- gate_z: bfloat16 [4, 8192, 4096], P('dp', 'ctx'), may hold values from -40 to 40
- skip_d: float32 [64], replicated, may hold values from 0.5 to 2
- norm_gain: float32 [4096], replicated, may hold values from 0.25 to 1.75
- query: bfloat16 [4, 8192, 4096], P('dp', 'ctx'), may hold values from -5 to 5
- key: bfloat16 [4, 8192, 1024], P('dp', 'ctx'), may hold values from -5 to 5
- value: bfloat16 [4, 8192, 1024], P('dp', 'ctx'), may hold values from -12 to 12
- loss_weight: float32 [4, 8192], P('dp', 'ctx'), may hold values from 1 to 90
Outputs:
- mamba_mix: bfloat16 [4, 8192, 4096], P('dp', 'ctx')
- attn_mix: bfloat16 [4, 8192, 4096], P('dp', 'ctx')
- energy: float32 [2, 2], replicated
The draws below stay inside these ranges and needn't reach their ends.
Inputs may be any that keep to these rules, and one draw needn't show every extreme that they name: `doc_start`: the documents of a sequence tile its positions in order: the first starts at 0, each ends where the next starts, the last ends at 8192. Each document has 1 to 384 positions, and every sequence has a document of exactly 384 positions. doc_end of a document is doc_start of the next one. `log_decay`: Negative.
All inputs are finite; a program needn't handle non-finite values.
Results may differ from the reference program's by a relative error of at most 0.0065.
Values may be sent and summed in bfloat16 or wider, within the bound.
A program may use at most 320 MiB of HBM per device.

```python
import math
import jax
import jax.numpy as jnp
from jax import lax

H = 64
P_SIZE = 64
N = 128
NG = 4
AQ = 32
AK = 8
AD = 128
TOK_DEV = 128
REACH = 3
GROUPS = 4
SEQ = 8192
DOCS = 64
N_CTX = 64


steep_total = 4.2


hush_factor = 0.0001


def document_bounds(key):
    base = jax.random.fold_in(key, 101)
    key_weight, key_place = jax.random.split(base)
    longest = REACH * TOK_DEV
    spare = SEQ - longest - (DOCS - 1)
    weights = jax.random.randint(key_weight, (GROUPS, DOCS - 1), 500, 1001)
    total = jnp.sum(weights, axis=1, keepdims=True)
    extra = weights * spare // total
    leftover = spare - jnp.sum(extra, axis=1, keepdims=True)
    order = jnp.arange(DOCS - 1, dtype=jnp.int32)[None, :]
    smaller = 1 + extra + (order < leftover).astype(jnp.int32)
    place = jax.random.randint(key_place, (GROUPS, 1), 0, DOCS)
    slots = jnp.broadcast_to(jnp.arange(DOCS, dtype=jnp.int32)[None, :], (GROUPS, DOCS))
    same_index = jnp.take_along_axis(smaller, jnp.clip(slots, 0, DOCS - 2), axis=1)
    prior_index = jnp.take_along_axis(smaller, jnp.clip(slots - 1, 0, DOCS - 2), axis=1)
    lengths = jnp.where(slots < place, same_index, jnp.where(slots == place, longest, prior_index))
    ends = jnp.cumsum(lengths, axis=1).astype(jnp.int32)
    begins = (ends - lengths).astype(jnp.int32)
    long_begin = jnp.sum(jnp.where(slots == place, begins, 0), axis=1).astype(jnp.int32)
    return (begins, ends, long_begin)


def draw_doc_start(key, part):
    return document_bounds(key)[0]


def draw_doc_end(key, part):
    return document_bounds(key)[1]


def long_spans(key):
    long_begin = document_bounds(key)[2]
    positions = jnp.arange(SEQ, dtype=jnp.int32)[None, :]
    first_block = long_begin[:, None] // TOK_DEV
    steep_block = positions // TOK_DEV == first_block + 1
    hushed_span = (positions >= (first_block + 1) * TOK_DEV) & (positions < long_begin[:, None] + REACH * TOK_DEV)
    return (steep_block, hushed_span)


def decay_law(key):
    keys = jax.random.split(jax.random.fold_in(key, 202), 7)
    share_fast = 0.5
    fast = jax.random.uniform(keys[0], (H,)) < share_fast
    slow_rate = jnp.exp(jax.random.uniform(keys[1], (H,), minval=math.log(0.05), maxval=math.log(1.0))) / (REACH * TOK_DEV)
    quick_rate = jnp.exp(jax.random.uniform(keys[2], (H,), minval=math.log(1.0 / 50), maxval=math.log(1.0 / 30)))
    rate = jnp.where(fast, quick_rate, slow_rate)
    blocks = jnp.exp(jax.random.uniform(keys[3], (GROUPS, H, SEQ // TOK_DEV), minval=math.log(0.5), maxval=math.log(2.0)))
    blockwise = jnp.repeat(blocks, TOK_DEV, axis=2)
    rough = jnp.exp(jax.random.uniform(keys[4], (GROUPS, H, SEQ), minval=math.log(0.5), maxval=math.log(2.0)))
    spots = jax.random.randint(keys[5], (GROUPS, 4), 0, SEQ)
    positions = jnp.arange(SEQ, dtype=jnp.int32)
    struck = jnp.any(positions[None, :, None] == spots[:, None, :], axis=2).astype(jnp.float32)
    depth = jax.random.uniform(keys[6], (GROUPS, H, SEQ), minval=math.log(1.25), maxval=math.log(2.0))
    drawn = -rate[None, :, None] * blockwise * rough - struck[:, None, :] * depth
    steep_block, hushed_span = long_spans(key)
    steep_rate = -(steep_total / TOK_DEV) * rough
    shaped = jnp.where(steep_block[:, None, :], steep_rate, drawn)
    return jnp.maximum(shaped, -1.0)


def draw_log_decay(key, part):
    return decay_law(key)


def draw_x_in(key, part):
    decay = decay_law(key)
    scale = jnp.sqrt(-jnp.expm1(2.0 * decay))
    noise_key = jax.random.fold_in(key, 303)
    raw = jnp.clip(jax.random.normal(noise_key, (GROUPS, SEQ, H, P_SIZE)), -5.0, 5.0)
    steep_block, hushed_span = long_spans(key)
    damping = jnp.where(hushed_span, hush_factor, 1.0)[:, :, None, None]
    shaped = raw * jnp.transpose(scale, (0, 2, 1))[..., None] * damping
    return shaped.reshape(GROUPS, SEQ, H * P_SIZE).astype(jnp.bfloat16)


def draw_gate_z(key, part):
    key_val, key_row, key_col = jax.random.split(jax.random.fold_in(key, 606), 3)
    half = 0.5 * math.log(10.0)
    rows = jnp.exp(jax.random.uniform(key_row, (GROUPS, SEQ, 1), minval=0.0, maxval=half))
    cols = jnp.exp(jax.random.uniform(key_col, (1, 1, H * P_SIZE), minval=0.0, maxval=half))
    raw = jnp.clip(jax.random.normal(key_val, (GROUPS, SEQ, H * P_SIZE)), -4.0, 4.0)
    return (raw * rows * cols).astype(jnp.bfloat16)


def attention_inputs(key):
    keys = jax.random.split(jax.random.fold_in(key, 404), 2)
    ratio = AQ // AK
    queries = jnp.clip(1.3 * jax.random.normal(keys[0], (GROUPS, SEQ, AK, ratio, AD)), -5.0, 5.0)
    keyed = jnp.clip(1.3 * jax.random.normal(keys[1], (GROUPS, SEQ, AK, AD)), -5.0, 5.0)
    return (queries.reshape(GROUPS, SEQ, AQ * AD), keyed.reshape(GROUPS, SEQ, AK * AD))


def draw_query(key, part):
    return attention_inputs(key)[0].astype(jnp.bfloat16)


def draw_key(key, part):
    return attention_inputs(key)[1].astype(jnp.bfloat16)


def draw_loss_weight(key, part):
    noise_key = jax.random.fold_in(key, 505)
    groups_at = jnp.arange(GROUPS, dtype=jnp.float32)[:, None]
    places_at = jnp.arange(SEQ, dtype=jnp.float32)[None, :]
    rising = (1.0 + 2.0 * groups_at / max(GROUPS - 1, 1)) * (1.0 + 2.0 * places_at / max(SEQ - 1, 1))
    spread = jnp.exp(jax.random.uniform(noise_key, (GROUPS, SEQ), minval=0.0, maxval=math.log(10.0)))
    return spread * rising


def touch_ends(drawn, key, low, top_value):
    spot = [jax.random.randint(jax.random.fold_in(key, axis), (), 0, length) for axis, length in enumerate(drawn.shape)]
    widest = drawn.shape.index(max(drawn.shape))
    next_to = spot[:widest] + [(spot[widest] + 1) % drawn.shape[widest]] + spot[widest + 1:]
    return drawn.at[tuple(spot)].set(low).at[tuple(next_to)].set(top_value)


def level_of(rng, dims, cuts, low, largest):
    def one(position, shards_of):
        steps = jax.random.uniform(jax.random.fold_in(jax.random.fold_in(rng, 6), position), (shards_of,), jnp.float32, low / len(cuts), largest / len(cuts))
        return jnp.repeat(jnp.exp(steps), dims[position] // shards_of).reshape((-1,) + (1,) * (len(dims) - position - 1))

    factor_of = one(*cuts[0])
    for cut in cuts[1:]:
        factor_of = factor_of * one(*cut)
    return factor_of


def normal_values(key, dims, scale, limit, cuts=(), kind=jnp.bfloat16):
    values = scale * jax.random.normal(key, dims, jnp.float32)
    if cuts:
        values = values * level_of(key, dims, cuts, -0.22, 0.18)
    return jnp.clip(values, -limit, limit).astype(kind)


def setup_inputs(seed: int = 0) -> dict:
    arg_keys = jax.random.split(jax.random.key(seed), 15)
    return {
        "doc_start": draw_doc_start(jax.random.fold_in(arg_keys[14], 71), 0),
        "doc_end": draw_doc_end(jax.random.fold_in(arg_keys[14], 71), 0),
        "modality": touch_ends(jax.random.randint(arg_keys[2], (GROUPS, DOCS), 0, 2), jax.random.fold_in(arg_keys[2], 1), 0, 1).astype(jnp.int32),
        "x_in": draw_x_in(jax.random.fold_in(arg_keys[14], 71), 0),
        "log_decay": draw_log_decay(jax.random.fold_in(arg_keys[14], 71), 0),
        "b_in": normal_values(arg_keys[5], (GROUPS, SEQ, NG * N), 0.3, 2.5, ((0, 4), (1, 64))),
        "c_in": normal_values(arg_keys[6], (GROUPS, SEQ, NG * N), 0.3, 2.5, ((0, 4), (1, 64))),
        "gate_z": draw_gate_z(jax.random.fold_in(arg_keys[14], 71), 0),
        "skip_d": jnp.clip(jnp.exp(jax.random.uniform(arg_keys[8], (H,), jnp.float32, math.log(0.5), math.log(2.0))), 0.5, 2.0),
        "norm_gain": jnp.clip(1.0 + 0.15 * jax.random.normal(arg_keys[9], (H * P_SIZE,), jnp.float32), 0.25, 1.75),
        "query": draw_query(jax.random.fold_in(arg_keys[14], 71), 0),
        "key": draw_key(jax.random.fold_in(arg_keys[14], 71), 0),
        "value": normal_values(arg_keys[12], (GROUPS, SEQ, AK * AD), 2.0, 12.0, ((0, 4), (1, 64))),
        "loss_weight": draw_loss_weight(jax.random.fold_in(arg_keys[14], 71), 0),
    }


norm_eps = 1e-05
masked_score = -1e+30

def doc_lookup(starts, ends, modes, positions):
    inside = (positions[:, None] >= starts[None, :]) & (positions[:, None] < ends[None, :])
    member = inside.astype(jnp.int32)
    labels = jnp.arange(starts.shape[0], dtype=jnp.int32)
    doc_of = lax.optimization_barrier(jnp.sum(member * labels[None, :], axis=1))
    start_of = lax.optimization_barrier(jnp.sum(member * starts[None, :], axis=1))
    mode_of = lax.optimization_barrier(jnp.sum(member * modes[None, :], axis=1))
    present = lax.optimization_barrier(jnp.sum(member, axis=1)) > 0
    return (doc_of, start_of, mode_of, present)

def mamba_local(x_rows, decay_rows, b_rows, c_rows, doc_of):
    steps = x_rows.shape[0]
    per_group = H // NG
    running = jnp.cumsum(decay_rows, axis=1)
    order = jnp.arange(steps, dtype=jnp.int32)
    same_doc = (doc_of[:, None] == doc_of[None, :]) & (order[None, :] <= order[:, None])
    spread = running[:, :, None] - running[:, None, :]
    kernel = jnp.where(same_doc[None], jnp.exp(jnp.where(same_doc[None], spread, 0.0)), 0.0)
    b_grp = b_rows.reshape(steps, NG, N).astype(jnp.float32)
    c_grp = c_rows.reshape(steps, NG, N).astype(jnp.float32)
    intersection = jnp.einsum('tgn,sgn->gts', c_grp, b_grp)
    mixing = (kernel.reshape(NG, per_group, steps, steps) * intersection[:, None]).astype(jnp.bfloat16)
    x_grp = x_rows.reshape(steps, NG, per_group, P_SIZE).astype(jnp.float32)
    inner = jnp.einsum('ghts,sghp->tghp', mixing.astype(jnp.float32), x_grp)
    last_doc = doc_of == doc_of[steps - 1]
    tail = jnp.where(last_doc[None, :], jnp.exp(running[:, steps - 1:] - running), 0.0)
    tail_rows = tail.reshape(NG, per_group, steps).transpose(2, 0, 1)[..., None]
    weighted = (x_grp * tail_rows).astype(jnp.bfloat16)
    end_state = jnp.einsum('sghp,sgn->ghpn', weighted.astype(jnp.float32), b_grp)
    return (inner, end_state.reshape(H, P_SIZE, N), running)

def mamba_finish(inner, state_in, running, carried, c_rows, x_rows, skip_d, gate_rows, norm_gain):
    steps = x_rows.shape[0]
    per_group = H // NG
    c_wide = c_rows.reshape(steps, NG, N).astype(jnp.float32)
    reached = jnp.einsum('tgn,ghpn->tghp', c_wide, state_in.reshape(NG, per_group, P_SIZE, N), precision=lax.Precision.HIGHEST)
    factor = (jnp.exp(running) * carried[None, :]).T.reshape(steps, NG, per_group)[..., None]
    x_wide = x_rows.reshape(steps, NG, per_group, P_SIZE).astype(jnp.float32)
    result = inner + reached * factor + skip_d.reshape(NG, per_group)[None, :, :, None] * x_wide
    gated = result.reshape(steps, NG, per_group * P_SIZE) * jax.nn.silu(gate_rows.reshape(steps, NG, per_group * P_SIZE).astype(jnp.float32))
    square = lax.optimization_barrier(jnp.mean(gated * gated, axis=-1, keepdims=True))
    normed = gated * lax.rsqrt(square + norm_eps) * norm_gain.reshape(NG, per_group * P_SIZE)[None]
    return normed.reshape(steps, H * P_SIZE).astype(jnp.bfloat16)

def normalize(scores, allowed):
    scores = jnp.where(allowed[None], scores, masked_score)
    top = lax.optimization_barrier(jnp.max(scores, axis=-1, keepdims=True))
    expo = jnp.exp(scores - top)
    return (expo / lax.optimization_barrier(jnp.sum(expo, axis=-1, keepdims=True))).astype(jnp.bfloat16)

def attend(query_rows, keys_all, values_all, allowed):
    ratio = AQ // AK
    steps = query_rows.shape[0]
    scale = AD ** (-0.5)
    q_heads = query_rows.reshape(steps, AK, ratio, AD).transpose(1, 2, 0, 3).astype(jnp.float32)
    k_heads = keys_all.reshape(-1, AK, AD).transpose(1, 0, 2).astype(jnp.float32)
    v_heads = values_all.reshape(-1, AK, AD).transpose(1, 0, 2).astype(jnp.float32)

    def per_head(operands):
        scores = jnp.einsum('rtd,kd->rtk', operands[0], operands[1]) * scale
        probs = normalize(scores, allowed)
        return jnp.einsum('rtk,kd->rtd', probs.astype(jnp.float32), operands[2])
    heads_out = lax.map(per_head, (q_heads, k_heads, v_heads))
    return heads_out.transpose(2, 0, 1, 3).reshape(steps, AQ * AD).astype(jnp.bfloat16)

def reference(doc_start, doc_end, modality, x_in, log_decay, b_in, c_in, gate_z, skip_d, norm_gain, query, key, value, loss_weight):
    margin = REACH * TOK_DEV
    window = (2 * REACH + 1) * TOK_DEV
    count = float(GROUPS * SEQ)
    mamba_list = []
    attn_list = []
    energy = jnp.zeros((2, 2), jnp.float32)
    for group in range(GROUPS):
        starts = doc_start[group]
        ends = doc_end[group]
        modes = modality[group]
        key_pad = jnp.pad(key[group], ((margin, margin), (0, 0)))
        value_pad = jnp.pad(value[group], ((margin, margin), (0, 0)))

        def block_step(state, block):
            first = (block * TOK_DEV).astype(jnp.int32)
            positions = first + jnp.arange(TOK_DEV, dtype=jnp.int32)
            x_rows = lax.dynamic_slice_in_dim(x_in[group], first, TOK_DEV, 0)
            decay_rows = lax.dynamic_slice_in_dim(log_decay[group], first, TOK_DEV, 1)
            b_rows = lax.dynamic_slice_in_dim(b_in[group], first, TOK_DEV, 0)
            c_rows = lax.dynamic_slice_in_dim(c_in[group], first, TOK_DEV, 0)
            gate_rows = lax.dynamic_slice_in_dim(gate_z[group], first, TOK_DEV, 0)
            query_rows = lax.dynamic_slice_in_dim(query[group], first, TOK_DEV, 0)
            weight_rows = lax.dynamic_slice_in_dim(loss_weight[group], first, TOK_DEV, 0)
            doc_of, start_of, mode_of, present = doc_lookup(starts, ends, modes, positions)
            inner, end_state, running = mamba_local(x_rows, decay_rows, b_rows, c_rows, doc_of)
            carried = (start_of < first).astype(jnp.float32)
            through = jnp.exp(running[:, TOK_DEV - 1]) * carried[TOK_DEV - 1]
            mixed = mamba_finish(inner, state, running, carried, c_rows, x_rows, skip_d, gate_rows, norm_gain)
            new_state = through[:, None, None] * state + end_state
            keys_all = lax.dynamic_slice_in_dim(key_pad, first, window, 0)
            values_all = lax.dynamic_slice_in_dim(value_pad, first, window, 0)
            key_pos = first - margin + jnp.arange(window, dtype=jnp.int32)
            key_doc, key_start, key_mode, key_present = doc_lookup(starts, ends, modes, key_pos)
            allowed = key_present[None, :] & (doc_of[:, None] == key_doc[None, :]) & ((key_pos[None, :] <= positions[:, None]) | (mode_of[:, None] == 1))
            attended = attend(query_rows, keys_all, values_all, allowed)
            mamba_energy = lax.optimization_barrier(jnp.mean(jnp.square(mixed.astype(jnp.float32)), axis=-1))
            attn_energy = lax.optimization_barrier(jnp.mean(jnp.square(attended.astype(jnp.float32)), axis=-1))
            mode_hot = jnp.stack([mode_of == 0, mode_of == 1]).astype(jnp.float32) * weight_rows[None, :]
            terms = jnp.stack([lax.optimization_barrier(jnp.sum(mode_hot * mamba_energy[None, :], axis=1)), lax.optimization_barrier(jnp.sum(mode_hot * attn_energy[None, :], axis=1))], axis=1) / count
            return (new_state, (mixed, attended, terms))
        final_state, outputs = lax.scan(block_step, jnp.zeros((H, P_SIZE, N), jnp.float32), jnp.arange(N_CTX, dtype=jnp.int32))
        mamba_list.append(outputs[0].reshape(SEQ, H * P_SIZE))
        attn_list.append(outputs[1].reshape(SEQ, AQ * AD))
        energy = energy + lax.optimization_barrier(jnp.sum(outputs[2], axis=0))
    return (jnp.stack(mamba_list), jnp.stack(attn_list), energy)
```

```python
import functools
import math

import jax
import jax.numpy as jnp
from jax import lax
from jax.experimental import pallas as pl
from jax.experimental.pallas import tpu as pltpu
from jax.sharding import PartitionSpec as P

H = 64
P_SIZE = 64
N = 128
NG = 4
AQ = 32
AK = 8
AD = 128
REACH = 3
TOK = 128
WIN = (2 * REACH + 1) * TOK
GW = (H // NG) * P_SIZE
HPG = H // NG

norm_eps = 1e-05
masked_score = -1e30
MESH = pl.DeviceIdType.MESH
HIGHEST = lax.Precision.HIGHEST
f32 = jnp.float32
bf16 = jnp.bfloat16
NT = (((1,), (1,)), ((), ()))
TN = (((0,), (0,)), ((), ()))
NN = (((1,), (0,)), ((), ()))


def dot(a, b, dims=NN, precision=None):
    return lax.dot_general(a, b, dims, precision=precision, preferred_element_type=f32)


def iota(shape, axis):
    return lax.broadcasted_iota(jnp.int32, shape, axis)


def body(
    n_dp,
    n_ctx,
    near,
    starts_ref,
    ends_ref,
    modes_ref,
    x_ref,
    decay_ref,
    b_ref,
    c_ref,
    gate_ref,
    skip_ref,
    gain_ref,
    q_ref,
    k_ref,
    v_ref,
    lw_ref,
    mamba_ref,
    attn_ref,
    energy_ref,
    kbuf,
    vbuf,
    abuf,
    bbuf,
    sbuf,
    ebuf,
    ewide,
    tbuf,
    tsend,
    fx,
    res,
    bias,
    mmask,
    lastm,
    carm,
    hot,
    runc,
    runr,
    acc,
    lsum,
    mtop,
    esq,
    e1,
    e2,
    e3,
    kv_send,
    kv_recv,
    st_send,
    a_recv,
    b_recv,
    s_send,
    s_recv,
    rel1,
    rel2,
    en_send,
    en_recv,
):
    b = lax.axis_index("ctx")
    dp = lax.axis_index("dp")
    core = b % 2
    row, lane_pos = b // near, b % near
    n_row = n_ctx // near
    seq = n_ctx * TOK
    first = b * TOK
    even, odd = core == 0, core == 1

    def peer(i):
        return {"ctx": i}

    barrier = pltpu.get_barrier_semaphore()

    def greet(device):
        pl.semaphore_signal(barrier, inc=1, device_id=device, device_id_type=MESH)

    @pl.loop(1, near)
    def _(k):
        greet({"ctx": row * near + (lane_pos + k) % near})

    for k in range(1, n_row):
        greet({"ctx": ((row + k) % n_row) * near + lane_pos})
    for k in range(1, n_dp):
        greet({"dp": (dp + k) % n_dp})
    count = near - 1 + n_row - 1 + n_dp - 1
    for d in (-2, -1, 1, 2):
        ok = (b + d >= 0) & (b + d < n_ctx)

        @pl.when(ok)
        def _(d=d):
            greet({"ctx": b + d})

        count = count + jnp.where(ok, 1, 0)

    st_row = starts_ref[...].astype(f32)
    en_row = ends_ref[...].astype(f32)
    mo_row = modes_ref[...].astype(f32)
    docs = st_row.shape[1]
    diag = iota((docs, docs), 0) == iota((docs, docs), 1)

    def column(r):
        return jnp.sum(jnp.where(diag, r, 0.0), axis=1, keepdims=True)

    st_col, en_col, mo_col = column(st_row), column(en_row), column(mo_row)
    first_f = first.astype(f32)
    pos_col = first_f + iota((TOK, 1), 0).astype(f32)
    below = st_row <= pos_col
    member = jnp.where(below & (pos_col < en_row), 1.0, 0.0)
    cnt_col = jnp.sum(jnp.where(below, 1.0, 0.0), axis=1, keepdims=True)
    begin_col = jnp.sum(member * st_row, axis=1, keepdims=True)
    mode_col = jnp.sum(member * mo_row, axis=1, keepdims=True)
    key_pos = first_f - float(REACH * TOK) + iota((1, WIN), 1).astype(f32)
    cnt_row = jnp.sum(jnp.where(st_col <= key_pos, 1.0, 0.0), axis=0, keepdims=True)
    present = (key_pos >= 0.0) & (key_pos < float(seq))
    same = (cnt_row == cnt_col) & present
    allowed = same & ((key_pos <= pos_col) | (mode_col == 1.0))
    bias[...] = jnp.where(allowed, 0.0, masked_score)
    own = slice(REACH * TOK, (REACH + 1) * TOK)
    own_same = cnt_row[:, own] == cnt_col
    mmask[...] = jnp.where(own_same & (iota((TOK, TOK), 1) <= iota((TOK, TOK), 0)), 1.0, 0.0)
    lastm[...] = jnp.broadcast_to(
        jnp.where(cnt_col == cnt_col[TOK - 1 :, :], 1.0, 0.0), (TOK, TOK)
    )
    carried = jnp.where(begin_col < first_f, 1.0, 0.0)
    carm[...] = jnp.broadcast_to(carried, (TOK, TOK))
    own_pos = key_pos[:, own]
    own_member = jnp.where((st_col <= own_pos) & (own_pos < en_col), 1.0, 0.0)
    mode_row = jnp.sum(own_member * mo_col, axis=0, keepdims=True)
    which = iota((8, TOK), 0).astype(f32)
    hot[...] = jnp.where(which == mode_row, lw_ref[...], 0.0)

    upto = jnp.where(iota((TOK, TOK), 0) >= iota((TOK, TOK), 1), 1.0, 0.0)
    decay = decay_ref[...]
    runr[...] = dot(decay, upto, NT, HIGHEST)
    for g in range(NG):
        runc[g, :, :HPG] = dot(upto, decay[g * HPG : (g + 1) * HPG, :], NT, HIGHEST)
    esq[...] = jnp.zeros_like(esq)

    for i in (0, 1, 2, 4, 5, 6):

        @pl.when((b - REACH + i < 0) | (b - REACH + i >= n_ctx))
        def _(i=i):
            kbuf[i] = jnp.zeros((TOK, AK * AD), bf16)
            vbuf[i] = jnp.zeros((TOK, AK * AD), bf16)

    @pl.when(b == 0)
    def _():
        abuf[...] = jnp.zeros_like(abuf)
        sbuf[...] = jnp.zeros_like(sbuf)

    @pl.when(b < 3)
    def _():
        bbuf[...] = jnp.zeros_like(bbuf)

    pl.semaphore_wait(barrier, count)

    def remote(src, dst, send, recv, to):
        return pltpu.make_async_remote_copy(
            src_ref=src,
            dst_ref=dst,
            send_sem=send,
            recv_sem=recv,
            device_id=peer(to),
            device_id_type=MESH,
        )

    def kv(which_send, from_slot, to_slot, to):
        k_src = k_ref if from_slot is None else kbuf.at[from_slot]
        v_src = v_ref if from_slot is None else vbuf.at[from_slot]
        return (
            remote(k_src, kbuf.at[to_slot], kv_send.at[which_send, 0], kv_recv.at[to_slot, 0], to),
            remote(v_src, vbuf.at[to_slot], kv_send.at[which_send, 1], kv_recv.at[to_slot, 1], to),
        )

    fwd2, bwd2 = b + 2 < n_ctx, b - 2 >= 0
    fwd1, bwd1 = b + 1 < n_ctx, b - 1 >= 0
    has_r2, has_l2 = bwd2, fwd2
    sends = [
        (fwd2, lambda: kv(0, None, 1, b + 2)),
        (bwd2, lambda: kv(1, None, 5, b - 2)),
        (even, lambda: kv(2, None, 2, b + 1)),
        (odd, lambda: kv(2, None, 4, b - 1)),
    ]
    relays = [
        (has_r2 & even, lambda: kv(3, 1, 0, b + 1)),
        (has_r2 & odd, lambda: kv(3, 1, 2, b - 1)),
        (has_l2 & even, lambda: kv(4, 5, 4, b + 1)),
        (has_l2 & odd, lambda: kv(4, 5, 6, b - 1)),
        (has_r2 & odd & fwd1, lambda: kv(5, 1, 0, b + 1)),
        (has_l2 & even & bwd1, lambda: kv(5, 5, 6, b - 1)),
    ]

    def start(plan):
        for when, make in plan:

            @pl.when(when)
            def _(make=make):
                for copy in make():
                    copy.start()

    def sent(plan):
        for when, make in plan:

            @pl.when(when)
            def _(make=make):
                for copy in make():
                    copy.wait_send()

    def arrived(slot):
        @pl.when((b - REACH + slot >= 0) & (b - REACH + slot < n_ctx))
        def _():
            for copy in kv(0, None, slot, b):
                copy.wait_recv()

    start(sends)

    lane = iota((TOK, TOK), 1)
    left = lane < P_SIZE

    def state_copy(g):
        return remote(ebuf.at[g], abuf.at[g], st_send.at[g], a_recv.at[g], b + 1)

    def scale_copy():
        return remote(tsend, sbuf, s_send, s_recv, b + 1)

    @pl.loop(0, NG)
    def _(g):
        cols = runc[g]
        parts = []
        for pair in range(HPG // 2):
            at = slice(pair * TOK, (pair + 1) * TOK)
            c0 = jnp.broadcast_to(cols[:, 2 * pair : 2 * pair + 1], (TOK, TOK))
            c1 = jnp.broadcast_to(cols[:, 2 * pair + 1 : 2 * pair + 2], (TOK, TOK))
            both = jnp.where(left, c0, c1)
            end = both[TOK - 1 :, :]
            fx[g, :, at] = jnp.exp(both) * carm[...]
            tbuf[g, :, at] = jnp.exp(end) * carm[TOK - 1 :, :]
            tail = jnp.exp(end - both) * lastm[...]
            lanes = pl.ds(pl.multiple_of(g * GW + pair * TOK, TOK), TOK)
            parts.append((x_ref[:, lanes].astype(f32) * tail).astype(bf16))
        weighted = jnp.concatenate(parts, axis=1)
        b_grp = b_ref[:, pl.ds(pl.multiple_of(g * N, N), N)]
        e = dot(b_grp, weighted, TN)
        ewide[g] = e
        ebuf[g] = e.astype(bf16)

        @pl.when(even)
        def _():
            state_copy(g).start()

    @pl.when(even)
    def _():
        tsend[...] = tbuf[...]
        scale_copy().start()

    @pl.when(odd)
    def _():
        scale_copy().wait_recv()
        tsend[...] = tbuf[...] * sbuf[...]

        @pl.when(fwd1)
        def _():
            scale_copy().start()

    def combine(g):
        state_copy(g).wait_recv()
        ebuf[g] = (ewide[g] + tbuf[g] * abuf[g].astype(f32)).astype(bf16)

        @pl.when(fwd1)
        def _():
            state_copy(g).start()

    @pl.when(odd)
    def _():
        combine(0)
        combine(1)

    @pl.loop(0, NG)
    def _(g):
        lanes_n = pl.ds(pl.multiple_of(g * N, N), N)
        both_docs = dot(c_ref[:, lanes_n], b_ref[:, lanes_n], NT) * mmask[...]
        cols = runc[g]
        rows = runr[pl.ds(pl.multiple_of(g * HPG, HPG), HPG), :]
        for pair in range(HPG // 2):
            at = slice(pair * TOK, (pair + 1) * TOK)
            mixes = []
            for h in (2 * pair, 2 * pair + 1):
                spread = cols[:, h : h + 1] - rows[h : h + 1, :]
                mixes.append((jnp.exp(jnp.minimum(spread, 0.0)) * both_docs).astype(bf16))
            xp = x_ref[:, pl.ds(pl.multiple_of(g * GW + pair * TOK, TOK), TOK)]
            zero = jnp.zeros_like(xp)
            split = jnp.concatenate([jnp.where(left, xp, zero), jnp.where(left, zero, xp)], axis=0)
            inner = dot(jnp.concatenate(mixes, axis=1), split)
            h0 = g * HPG + 2 * pair
            skip = jnp.where(left, skip_ref[h0], skip_ref[h0 + 1])
            res[g, :, at] = inner + skip * xp.astype(f32)

    arrived(1)
    arrived(5)
    start(relays)

    @pl.when(odd)
    def _():
        combine(2)
        combine(3)

    ratio = AQ // AK
    scale = AD ** (-0.5) * math.log2(math.e)

    def attend(j, slots):
        heads = pl.ds(pl.multiple_of(j * AD, AD), AD)
        q = jnp.concatenate(
            [
                q_ref[:, pl.ds(pl.multiple_of(j * ratio * AD + r * AD, AD), AD)]
                for r in range(ratio)
            ],
            axis=0,
        )
        keys = jnp.concatenate(
            [(k_ref[:, heads] if i == REACH else kbuf[i, :, heads]) for i in slots], axis=0
        )
        values = jnp.concatenate(
            [(v_ref[:, heads] if i == REACH else vbuf[i, :, heads]) for i in slots], axis=0
        )
        masks = jnp.concatenate([bias[:, i * TOK : (i + 1) * TOK] for i in slots], axis=1)
        s = dot(q, keys, NT) * scale
        s = s.reshape(ratio, TOK, len(slots) * TOK) + masks[None]
        s = s.reshape(ratio * TOK, len(slots) * TOK)
        wide = jnp.concatenate([values, jnp.ones_like(values)], axis=1)
        return s, wide

    near_slots, far_slots = (1, 2, 3, 4, 5), (0, 6)
    arrived(2)
    arrived(4)

    def relay_state(g):
        up = remote(abuf.at[g], bbuf.at[g], rel1.at[g], b_recv.at[g], b + 1)
        over = remote(abuf.at[g], bbuf.at[g], rel2.at[g], b_recv.at[g], b + 2)
        return up, over

    def pass_on(g):
        @pl.when(even & bwd1)
        def _():
            state_copy(g).wait_recv()
            up, over = relay_state(g)

            @pl.when(fwd2)
            def _():
                over.start()

            up.start()

    @pl.loop(0, NG)
    def _(g):
        for half in range(AK // NG):
            j = g * (AK // NG) + half
            s, wide = attend(j, near_slots)
            top = jnp.max(s, axis=1, keepdims=True)
            p = jnp.exp2(s - top).astype(bf16)
            o = dot(p, wide)
            acc[j] = o[:, :AD]
            lsum[j] = o[:, AD:]
            mtop[j] = jnp.broadcast_to(top, (ratio * TOK, AD))
        pass_on(g)

    arrived(0)
    arrived(6)

    @pl.loop(0, AK)
    def _(j):
        s, wide = attend(j, far_slots)
        before = mtop[j]
        top = jnp.maximum(before, jnp.max(s, axis=1, keepdims=True))
        p = jnp.exp2(s - jnp.concatenate([top] * len(far_slots), axis=1)).astype(bf16)
        o = dot(p, wide)
        fade = jnp.exp2(before - top)
        total = lsum[j] * fade + o[:, AD:]
        out = ((acc[j] * fade + o[:, :AD]) / total).astype(bf16)
        square = jnp.zeros((TOK, AD), f32)
        for r in range(ratio):
            piece = out[r * TOK : (r + 1) * TOK]
            attn_ref[:, pl.ds(pl.multiple_of(j * ratio * AD + r * AD, AD), AD)] = piece
            wide_piece = piece.astype(f32)
            square = square + wide_piece * wide_piece
        esq[1] = esq[1] + square

    @pl.when(odd)
    def _():
        pass

    @pl.when(even & bwd1)
    def _():
        scale_copy().wait_recv()

    @pl.loop(0, NG)
    def _(g):
        @pl.when(b >= 3)
        def _():
            remote(bbuf.at[g], bbuf.at[g], rel1.at[g], b_recv.at[g], b).wait_recv()

        c_grp = c_ref[:, pl.ds(pl.multiple_of(g * N, N), N)]
        reached = dot(c_grp, abuf[g]) + dot(c_grp, bbuf[g]) * sbuf[g]
        lanes = pl.ds(pl.multiple_of(g * GW, GW), GW)
        result = res[g] + reached * fx[g]
        z = gate_ref[:, lanes].astype(f32)
        gated = result * (z / (1.0 + jnp.exp(-z)))
        square = jnp.sum(gated * gated, axis=1, keepdims=True) * (1.0 / GW)
        mixed = (gated * lax.rsqrt(square + norm_eps) * gain_ref[:, lanes]).astype(bf16)
        mamba_ref[:, lanes] = mixed
        again = mixed.astype(f32)
        again = again * again
        part = again[:, :TOK]
        for i in range(1, GW // TOK):
            part = part + again[:, i * TOK : (i + 1) * TOK]
        esq[0] = esq[0] + part

    per_mode = [
        jnp.sum(dot(hot[...], esq[i], NN, HIGHEST), axis=1, keepdims=True) for i in range(2)
    ]
    small = iota((8, TOK), 1)
    denom = float(n_dp * n_ctx * TOK) * float(H * P_SIZE)
    mine = jnp.where(small == 0, per_mode[0], jnp.where(small == 1, per_mode[1], 0.0)) / denom

    def exchange(buf, size, me, base, device_of, value):
        buf[me] = value

        def copy(to_index, from_index):
            return pltpu.make_async_remote_copy(
                src_ref=buf.at[me],
                dst_ref=buf.at[from_index],
                send_sem=en_send.at[base + to_index],
                recv_sem=en_recv.at[base + from_index],
                device_id=device_of(to_index),
                device_id_type=MESH,
            )

        @pl.loop(1, size)
        def _(k):
            copy((me + k) % size, me).start()

        @pl.loop(1, size)
        def _(k):
            other = (me + k) % size
            copy(other, other).wait_recv()

        total = buf[0]
        for i in range(1, size):
            total = total + buf[i]
        return total, lambda k: copy((me + k) % size, me).wait_send()

    done = []
    value = mine
    plans = (
        (e1, near, lane_pos, 0, lambda i: {"ctx": row * near + i}),
        (e2, n_row, row, near, lambda i: {"ctx": i * near + lane_pos}),
        (e3, n_dp, dp, near + n_row, lambda i: {"dp": i}),
    )
    for buf, size, me, base, device_of in plans:
        if size > 1:
            value, wait = exchange(buf, size, me, base, device_of, value)
            done.append((size, wait))
    energy_ref[...] = value

    for size, wait in done:

        @pl.loop(1, size)
        def _(k, wait=wait):
            wait(k)

    sent(sends)
    sent(relays)

    @pl.when(even | fwd1)
    def _():
        scale_copy().wait_send()

        @pl.loop(0, NG)
        def _(g):
            state_copy(g).wait_send()

    @pl.when(even & bwd1)
    def _():
        @pl.loop(0, NG)
        def _(g):
            up, over = relay_state(g)
            up.wait_send()

            @pl.when(fwd2)
            def _():
                over.wait_send()


def shards(n_dp, n_ctx, near, *args):
    (starts, ends, modes, x, decay, b_in, c_in, gate, skip, gain, q, k, v, lw) = args
    operands = (
        starts,
        ends,
        modes,
        x[0],
        decay[0],
        b_in[0],
        c_in[0],
        gate[0],
        skip,
        gain.reshape(1, H * P_SIZE),
        q[0],
        k[0],
        v[0],
        lw,
    )
    vmem = pl.BlockSpec(memory_space=pltpu.VMEM)
    smem = pl.BlockSpec(memory_space=pltpu.SMEM)
    specs = [vmem] * 8 + [smem] + [vmem] * 5
    n_row = n_ctx // near
    V, D = pltpu.VMEM, pltpu.SemaphoreType.DMA
    ratio = AQ // AK
    scratch = [
        V((2 * REACH + 1, TOK, AK * AD), bf16),
        V((2 * REACH + 1, TOK, AK * AD), bf16),
        V((NG, N, GW), bf16),
        V((NG, N, GW), bf16),
        V((NG, 1, GW), f32),
        V((NG, N, GW), bf16),
        V((NG, N, GW), f32),
        V((NG, 1, GW), f32),
        V((NG, 1, GW), f32),
        V((NG, TOK, GW), f32),
        V((NG, TOK, GW), f32),
        V((TOK, WIN), f32),
        V((TOK, TOK), f32),
        V((TOK, TOK), f32),
        V((TOK, TOK), f32),
        V((8, TOK), f32),
        V((NG, TOK, TOK), f32),
        V((H, TOK), f32),
        V((AK, ratio * TOK, AD), f32),
        V((AK, ratio * TOK, AD), f32),
        V((AK, ratio * TOK, AD), f32),
        V((2, TOK, TOK), f32),
        V((near, 8, TOK), f32),
        V((n_row, 8, TOK), f32),
        V((n_dp, 8, TOK), f32),
        D((6, 2)),
        D((7, 2)),
        D((NG,)),
        D((NG,)),
        D((NG,)),
        D,
        D,
        D((NG,)),
        D((NG,)),
        D((near + n_row + n_dp,)),
        D((near + n_row + n_dp,)),
    ]
    mamba, attn, energy = pl.pallas_call(
        functools.partial(body, n_dp, n_ctx, near),
        out_shape=(
            jax.ShapeDtypeStruct((TOK, H * P_SIZE), bf16),
            jax.ShapeDtypeStruct((TOK, AQ * AD), bf16),
            jax.ShapeDtypeStruct((8, TOK), f32),
        ),
        in_specs=specs,
        out_specs=(vmem, vmem, vmem),
        scratch_shapes=scratch,
        compiler_params=pltpu.CompilerParams(
            collective_id=0, has_side_effects=True, vmem_limit_bytes=60 * 1024 * 1024
        ),
        name="mixers",
    )(*operands)
    return mamba[None], attn[None], energy[:2, :2]


def solution(mesh):
    placed = (
        P("dp", None),
        P("dp", None),
        P("dp", None),
        P("dp", "ctx", None),
        P("dp", None, "ctx"),
        P("dp", "ctx", None),
        P("dp", "ctx", None),
        P("dp", "ctx", None),
        P(),
        P(),
        P("dp", "ctx", None),
        P("dp", "ctx", None),
        P("dp", "ctx", None),
        P("dp", "ctx"),
    )
    n_dp, n_ctx = mesh.shape["dp"], mesh.shape["ctx"]
    return jax.shard_map(
        functools.partial(shards, n_dp, n_ctx, min(16, n_ctx)),
        mesh=mesh,
        in_specs=placed,
        out_specs=(P("dp", "ctx", None), P("dp", "ctx", None), P()),
        check_vma=False,
    )
```

```python
import functools
import math

import jax
import jax.numpy as jnp
from jax import lax
from jax.experimental import pallas as pl
from jax.experimental.pallas import tpu as pltpu
from jax.sharding import PartitionSpec as P

H = 64
P_SIZE = 64
N = 128
NG = 4
AQ = 32
AK = 8
AD = 128
REACH = 3
TOK = 128
WIN = (2 * REACH + 1) * TOK
GW = (H // NG) * P_SIZE
HPG = H // NG

norm_eps = 1e-05
masked_score = -1e30
MESH = pl.DeviceIdType.MESH
HIGHEST = lax.Precision.HIGHEST
f32 = jnp.float32
bf16 = jnp.bfloat16
NT = (((1,), (1,)), ((), ()))
TN = (((0,), (0,)), ((), ()))
NN = (((1,), (0,)), ((), ()))


def dot(a, b, dims=NN, precision=None):
    return lax.dot_general(a, b, dims, precision=precision, preferred_element_type=f32)


def iota(shape, axis):
    return lax.broadcasted_iota(jnp.int32, shape, axis)


def body(
    n_dp,
    n_ctx,
    near,
    starts_ref,
    ends_ref,
    modes_ref,
    x_hbm,
    decay_ref,
    b_hbm,
    c_hbm,
    gate_hbm,
    skip_ref,
    gain_ref,
    q_hbm,
    k_hbm,
    v_hbm,
    lw_ref,
    mamba_ref,
    attn_ref,
    energy_ref,
    x_ref,
    b_ref,
    c_ref,
    gate_ref,
    q_ref,
    kbuf,
    vbuf,
    abuf,
    bbuf,
    sbuf,
    ebuf,
    ewide,
    tbuf,
    tsend,
    fx,
    res,
    bias,
    mmask,
    lastm,
    carm,
    hot,
    runc,
    runr,
    acc,
    lsum,
    mtop,
    esq,
    e1,
    e2,
    kv_send,
    kv_recv,
    st_send,
    a_recv,
    b_recv,
    s_send,
    s_recv,
    rel1,
    rel2,
    en_send,
    en_recv,
    in_sem,
):
    b = lax.axis_index("ctx")
    dp = lax.axis_index("dp")
    core = b % 2
    row, lane_pos = b // near, b % near
    n_row = n_ctx // near
    seq = n_ctx * TOK
    first = b * TOK
    even, odd = core == 0, core == 1

    def peer(i):
        return {"ctx": i}

    barrier = pltpu.get_barrier_semaphore()

    def greet(device):
        pl.semaphore_signal(barrier, inc=1, device_id=device, device_id_type=MESH)

    @pl.loop(1, near)
    def _(k):
        greet({"ctx": row * near + (lane_pos + k) % near})

    columns = n_row * n_dp

    @pl.loop(1, columns)
    def _(k):
        i = (dp * n_row + row + k) % columns
        greet({"dp": i // n_row, "ctx": (i % n_row) * near + lane_pos})

    count = near - 1 + columns - 1
    for d in (-2, -1, 1, 2):
        ok = (b + d >= 0) & (b + d < n_ctx)

        @pl.when(ok)
        def _(d=d):
            greet({"ctx": b + d})

        count = count + jnp.where(ok, 1, 0)

    loads = [
        pltpu.make_async_copy(src, dst, in_sem.at[i])
        for i, (src, dst) in enumerate(
            (
                (x_hbm, x_ref),
                (b_hbm, b_ref),
                (c_hbm, c_ref),
                (k_hbm, kbuf.at[REACH]),
                (v_hbm, vbuf.at[REACH]),
                (q_hbm, q_ref),
                (gate_hbm, gate_ref),
            )
        )
    ]
    for load in loads:
        load.start()

    st_row = starts_ref[...].astype(f32)
    en_row = ends_ref[...].astype(f32)
    mo_row = modes_ref[...].astype(f32)
    docs = st_row.shape[1]
    diag = iota((docs, docs), 0) == iota((docs, docs), 1)

    def column(r):
        return jnp.sum(jnp.where(diag, r, 0.0), axis=1, keepdims=True)

    st_col, en_col, mo_col = column(st_row), column(en_row), column(mo_row)
    first_f = first.astype(f32)
    pos_col = first_f + iota((TOK, 1), 0).astype(f32)
    below = st_row <= pos_col
    member = jnp.where(below & (pos_col < en_row), 1.0, 0.0)
    cnt_col = jnp.sum(jnp.where(below, 1.0, 0.0), axis=1, keepdims=True)
    begin_col = jnp.sum(member * st_row, axis=1, keepdims=True)
    mode_col = jnp.sum(member * mo_row, axis=1, keepdims=True)
    key_pos = first_f - float(REACH * TOK) + iota((1, WIN), 1).astype(f32)
    cnt_row = jnp.sum(jnp.where(st_col <= key_pos, 1.0, 0.0), axis=0, keepdims=True)
    present = (key_pos >= 0.0) & (key_pos < float(seq))
    same = (cnt_row == cnt_col) & present
    allowed = same & ((key_pos <= pos_col) | (mode_col == 1.0))
    bias[...] = jnp.where(allowed, 0.0, masked_score)
    own = slice(REACH * TOK, (REACH + 1) * TOK)
    own_same = cnt_row[:, own] == cnt_col
    mmask[...] = jnp.where(own_same & (iota((TOK, TOK), 1) <= iota((TOK, TOK), 0)), 1.0, 0.0)
    lastm[...] = jnp.broadcast_to(
        jnp.where(cnt_col == cnt_col[TOK - 1 :, :], 1.0, 0.0), (TOK, TOK)
    )
    carried = jnp.where(begin_col < first_f, 1.0, 0.0)
    carm[...] = jnp.broadcast_to(carried, (TOK, TOK))
    own_pos = key_pos[:, own]
    own_member = jnp.where((st_col <= own_pos) & (own_pos < en_col), 1.0, 0.0)
    mode_row = jnp.sum(own_member * mo_col, axis=0, keepdims=True)
    which = iota((8, TOK), 0).astype(f32)
    hot[...] = jnp.where(which == mode_row, lw_ref[...], 0.0)

    upto = jnp.where(iota((TOK, TOK), 0) >= iota((TOK, TOK), 1), 1.0, 0.0)
    decay = decay_ref[...]
    runr[...] = dot(decay, upto, NT, HIGHEST)
    for g in range(NG):
        runc[g, :, :HPG] = dot(upto, decay[g * HPG : (g + 1) * HPG, :], NT, HIGHEST)
    esq[...] = jnp.zeros_like(esq)

    for i in (0, 1, 2, 4, 5, 6):

        @pl.when((b - REACH + i < 0) | (b - REACH + i >= n_ctx))
        def _(i=i):
            kbuf[i] = jnp.zeros((TOK, AK * AD), bf16)
            vbuf[i] = jnp.zeros((TOK, AK * AD), bf16)

    @pl.when(b == 0)
    def _():
        abuf[...] = jnp.zeros_like(abuf)
        sbuf[...] = jnp.zeros_like(sbuf)

    @pl.when(b < 3)
    def _():
        bbuf[...] = jnp.zeros_like(bbuf)

    pl.semaphore_wait(barrier, count)

    def remote(src, dst, send, recv, to):
        return pltpu.make_async_remote_copy(
            src_ref=src,
            dst_ref=dst,
            send_sem=send,
            recv_sem=recv,
            device_id=peer(to),
            device_id_type=MESH,
        )

    def kv(which_send, from_slot, to_slot, to):
        k_src = k_hbm if from_slot is None else kbuf.at[from_slot]
        v_src = v_hbm if from_slot is None else vbuf.at[from_slot]
        return (
            remote(k_src, kbuf.at[to_slot], kv_send.at[which_send, 0], kv_recv.at[to_slot, 0], to),
            remote(v_src, vbuf.at[to_slot], kv_send.at[which_send, 1], kv_recv.at[to_slot, 1], to),
        )

    fwd2, bwd2 = b + 2 < n_ctx, b - 2 >= 0
    fwd1, bwd1 = b + 1 < n_ctx, b - 1 >= 0
    has_r2, has_l2 = bwd2, fwd2
    sends = [
        (fwd2, lambda: kv(0, None, 1, b + 2)),
        (bwd2, lambda: kv(1, None, 5, b - 2)),
        (even, lambda: kv(2, None, 2, b + 1)),
        (odd, lambda: kv(2, None, 4, b - 1)),
    ]
    relays = [
        (has_r2 & even, lambda: kv(3, 1, 0, b + 1)),
        (has_r2 & odd, lambda: kv(3, 1, 2, b - 1)),
        (has_l2 & even, lambda: kv(4, 5, 4, b + 1)),
        (has_l2 & odd, lambda: kv(4, 5, 6, b - 1)),
        (has_r2 & odd & fwd1, lambda: kv(5, 1, 0, b + 1)),
        (has_l2 & even & bwd1, lambda: kv(5, 5, 6, b - 1)),
    ]

    def start(plan):
        for when, make in plan:

            @pl.when(when)
            def _(make=make):
                for copy in make():
                    copy.start()

    def sent(plan):
        for when, make in plan:

            @pl.when(when)
            def _(make=make):
                for copy in make():
                    copy.wait_send()

    def arrived(slot):
        @pl.when((b - REACH + slot >= 0) & (b - REACH + slot < n_ctx))
        def _():
            for copy in kv(0, None, slot, b):
                copy.wait_recv()

    start(sends)
    for load in loads[:3]:
        load.wait()

    lane = iota((TOK, TOK), 1)
    left = lane < P_SIZE

    def state_copy(g):
        return remote(ebuf.at[g], abuf.at[g], st_send.at[g], a_recv.at[g], b + 1)

    def scale_copy():
        return remote(tsend, sbuf, s_send, s_recv, b + 1)

    @pl.loop(0, NG)
    def _(g):
        cols = runc[g]
        parts = []
        for pair in range(HPG // 2):
            at = slice(pair * TOK, (pair + 1) * TOK)
            c0 = jnp.broadcast_to(cols[:, 2 * pair : 2 * pair + 1], (TOK, TOK))
            c1 = jnp.broadcast_to(cols[:, 2 * pair + 1 : 2 * pair + 2], (TOK, TOK))
            both = jnp.where(left, c0, c1)
            end = both[TOK - 1 :, :]
            fx[g, :, at] = jnp.exp(both) * carm[...]
            tbuf[g, :, at] = jnp.exp(end) * carm[TOK - 1 :, :]
            tail = jnp.exp(end - both) * lastm[...]
            lanes = pl.ds(pl.multiple_of(g * GW + pair * TOK, TOK), TOK)
            parts.append((x_ref[:, lanes].astype(f32) * tail).astype(bf16))
        weighted = jnp.concatenate(parts, axis=1)
        b_grp = b_ref[:, pl.ds(pl.multiple_of(g * N, N), N)]
        e = dot(b_grp, weighted, TN)
        ewide[g] = e
        ebuf[g] = e.astype(bf16)

        @pl.when(even)
        def _():
            state_copy(g).start()

    @pl.when(even)
    def _():
        tsend[...] = tbuf[...]
        scale_copy().start()

    @pl.when(odd)
    def _():
        scale_copy().wait_recv()
        tsend[...] = tbuf[...] * sbuf[...]

        @pl.when(fwd1)
        def _():
            scale_copy().start()

    def combine(g):
        state_copy(g).wait_recv()
        ebuf[g] = (ewide[g] + tbuf[g] * abuf[g].astype(f32)).astype(bf16)

        @pl.when(fwd1)
        def _():
            state_copy(g).start()

    @pl.when(odd)
    def _():
        combine(0)
        combine(1)

    @pl.loop(0, NG)
    def _(g):
        lanes_n = pl.ds(pl.multiple_of(g * N, N), N)
        both_docs = dot(c_ref[:, lanes_n], b_ref[:, lanes_n], NT) * mmask[...]
        cols = runc[g]
        rows = runr[pl.ds(pl.multiple_of(g * HPG, HPG), HPG), :]
        for pair in range(HPG // 2):
            at = slice(pair * TOK, (pair + 1) * TOK)
            mixes = []
            for h in (2 * pair, 2 * pair + 1):
                spread = cols[:, h : h + 1] - rows[h : h + 1, :]
                mixes.append((jnp.exp(jnp.minimum(spread, 0.0)) * both_docs).astype(bf16))
            xp = x_ref[:, pl.ds(pl.multiple_of(g * GW + pair * TOK, TOK), TOK)]
            zero = jnp.zeros_like(xp)
            split = jnp.concatenate([jnp.where(left, xp, zero), jnp.where(left, zero, xp)], axis=0)
            inner = dot(jnp.concatenate(mixes, axis=1), split)
            h0 = g * HPG + 2 * pair
            skip = jnp.where(left, skip_ref[h0], skip_ref[h0 + 1])
            res[g, :, at] = inner + skip * xp.astype(f32)

    arrived(1)
    arrived(5)
    start(relays)

    @pl.when(odd)
    def _():
        combine(2)
        combine(3)

    ratio = AQ // AK
    scale = AD ** (-0.5) * math.log2(math.e)

    def attend(j, slots):
        heads = pl.ds(pl.multiple_of(j * AD, AD), AD)
        q = jnp.concatenate(
            [
                q_ref[:, pl.ds(pl.multiple_of(j * ratio * AD + r * AD, AD), AD)]
                for r in range(ratio)
            ],
            axis=0,
        )
        keys = jnp.concatenate(
            [kbuf[i, :, heads] for i in slots], axis=0
        )
        values = jnp.concatenate(
            [vbuf[i, :, heads] for i in slots], axis=0
        )
        masks = jnp.concatenate([bias[:, i * TOK : (i + 1) * TOK] for i in slots], axis=1)
        s = dot(q, keys, NT) * scale
        s = s.reshape(ratio, TOK, len(slots) * TOK) + masks[None]
        s = s.reshape(ratio * TOK, len(slots) * TOK)
        wide = jnp.concatenate([values, jnp.ones_like(values)], axis=1)
        return s, wide

    for load in loads[3:]:
        load.wait()
    near_slots, far_slots = (1, 2, 3, 4, 5), (0, 6)
    arrived(2)
    arrived(4)

    def relay_state(g):
        up = remote(abuf.at[g], bbuf.at[g], rel1.at[g], b_recv.at[g], b + 1)
        over = remote(abuf.at[g], bbuf.at[g], rel2.at[g], b_recv.at[g], b + 2)
        return up, over

    def pass_on(g):
        @pl.when(even & bwd1)
        def _():
            state_copy(g).wait_recv()
            up, over = relay_state(g)

            @pl.when(fwd2)
            def _():
                over.start()

            up.start()

    @pl.loop(0, NG)
    def _(g):
        for half in range(AK // NG):
            j = g * (AK // NG) + half
            s, wide = attend(j, near_slots)
            top = jnp.max(s, axis=1, keepdims=True)
            p = jnp.exp2(s - top).astype(bf16)
            o = dot(p, wide)
            acc[j] = o[:, :AD]
            lsum[j] = o[:, AD:]
            mtop[j] = jnp.broadcast_to(top, (ratio * TOK, AD))
        pass_on(g)

    arrived(0)
    arrived(6)

    @pl.loop(0, AK)
    def _(j):
        s, wide = attend(j, far_slots)
        before = mtop[j]
        top = jnp.maximum(before, jnp.max(s, axis=1, keepdims=True))
        p = jnp.exp2(s - jnp.concatenate([top] * len(far_slots), axis=1)).astype(bf16)
        o = dot(p, wide)
        fade = jnp.exp2(before - top)
        total = lsum[j] * fade + o[:, AD:]
        out = ((acc[j] * fade + o[:, :AD]) / total).astype(bf16)
        square = jnp.zeros((TOK, AD), f32)
        for r in range(ratio):
            piece = out[r * TOK : (r + 1) * TOK]
            attn_ref[:, pl.ds(pl.multiple_of(j * ratio * AD + r * AD, AD), AD)] = piece
            wide_piece = piece.astype(f32)
            square = square + wide_piece * wide_piece
        esq[1] = esq[1] + square

    @pl.when(even & bwd1)
    def _():
        scale_copy().wait_recv()

    @pl.loop(0, NG)
    def _(g):
        @pl.when(b >= 3)
        def _():
            remote(bbuf.at[g], bbuf.at[g], rel1.at[g], b_recv.at[g], b).wait_recv()

        c_grp = c_ref[:, pl.ds(pl.multiple_of(g * N, N), N)]
        reached = dot(c_grp, abuf[g]) + dot(c_grp, bbuf[g]) * sbuf[g]
        lanes = pl.ds(pl.multiple_of(g * GW, GW), GW)
        result = res[g] + reached * fx[g]
        z = gate_ref[:, lanes].astype(f32)
        gated = result * (z / (1.0 + jnp.exp(-z)))
        square = jnp.sum(gated * gated, axis=1, keepdims=True) * (1.0 / GW)
        mixed = (gated * lax.rsqrt(square + norm_eps) * gain_ref[:, lanes]).astype(bf16)
        mamba_ref[:, lanes] = mixed
        again = mixed.astype(f32)
        again = again * again
        part = again[:, :TOK]
        for i in range(1, GW // TOK):
            part = part + again[:, i * TOK : (i + 1) * TOK]
        esq[0] = esq[0] + part

    per_mode = [
        jnp.sum(dot(hot[...], esq[i], NN, HIGHEST), axis=1, keepdims=True) for i in range(2)
    ]
    small = iota((8, TOK), 1)
    denom = float(n_dp * n_ctx * TOK) * float(H * P_SIZE)
    mine = jnp.where(small == 0, per_mode[0], jnp.where(small == 1, per_mode[1], 0.0)) / denom

    def exchange(buf, size, me, base, device_of, value):
        buf[me] = value

        def copy(to_index, from_index):
            return pltpu.make_async_remote_copy(
                src_ref=buf.at[me],
                dst_ref=buf.at[from_index],
                send_sem=en_send.at[base + to_index],
                recv_sem=en_recv.at[base + from_index],
                device_id=device_of(to_index),
                device_id_type=MESH,
            )

        @pl.loop(1, size)
        def _(k):
            copy((me + k) % size, me).start()

        @pl.loop(1, size)
        def _(k):
            other = (me + k) % size
            copy(other, other).wait_recv()

        total = buf[0]
        for i in range(1, size):
            total = total + buf[i]
        return total, lambda k: copy((me + k) % size, me).wait_send()

    done = []
    value = mine
    plans = (
        (e1, near, lane_pos, 0, lambda i: {"ctx": row * near + i}),
        (
            e2,
            n_row * n_dp,
            dp * n_row + row,
            near,
            lambda i: {"dp": i // n_row, "ctx": (i % n_row) * near + lane_pos},
        ),
    )
    for buf, size, me, base, device_of in plans:
        if size > 1:
            value, wait = exchange(buf, size, me, base, device_of, value)
            done.append((size, wait))
    energy_ref[...] = value[:2, :2]

    for size, wait in done:

        @pl.loop(1, size)
        def _(k, wait=wait):
            wait(k)

    sent(sends)
    sent(relays)

    @pl.when(even | fwd1)
    def _():
        scale_copy().wait_send()

        @pl.loop(0, NG)
        def _(g):
            state_copy(g).wait_send()

    @pl.when(even & bwd1)
    def _():
        @pl.loop(0, NG)
        def _(g):
            up, over = relay_state(g)
            up.wait_send()

            @pl.when(fwd2)
            def _():
                over.wait_send()


def shards(n_dp, n_ctx, near, *args):
    (starts, ends, modes, x, decay, b_in, c_in, gate, skip, gain, q, k, v, lw) = args
    operands = (
        starts,
        ends,
        modes,
        x[0],
        decay[0],
        b_in[0],
        c_in[0],
        gate[0],
        skip,
        gain.reshape(1, H * P_SIZE),
        q[0],
        k[0],
        v[0],
        lw,
    )
    vmem = pl.BlockSpec(memory_space=pltpu.VMEM)
    smem = pl.BlockSpec(memory_space=pltpu.SMEM)
    hbm = pl.BlockSpec(memory_space=pl.ANY)
    specs = [vmem] * 3 + [hbm, vmem, hbm, hbm, hbm, smem, vmem, hbm, hbm, hbm, vmem]
    n_row = n_ctx // near
    V, D = pltpu.VMEM, pltpu.SemaphoreType.DMA
    ratio = AQ // AK
    scratch = [
        V((TOK, H * P_SIZE), bf16),
        V((TOK, NG * N), bf16),
        V((TOK, NG * N), bf16),
        V((TOK, H * P_SIZE), bf16),
        V((TOK, AQ * AD), bf16),
        V((2 * REACH + 1, TOK, AK * AD), bf16),
        V((2 * REACH + 1, TOK, AK * AD), bf16),
        V((NG, N, GW), bf16),
        V((NG, N, GW), bf16),
        V((NG, 1, GW), f32),
        V((NG, N, GW), bf16),
        V((NG, N, GW), f32),
        V((NG, 1, GW), f32),
        V((NG, 1, GW), f32),
        V((NG, TOK, GW), f32),
        V((NG, TOK, GW), f32),
        V((TOK, WIN), f32),
        V((TOK, TOK), f32),
        V((TOK, TOK), f32),
        V((TOK, TOK), f32),
        V((8, TOK), f32),
        V((NG, TOK, TOK), f32),
        V((H, TOK), f32),
        V((AK, ratio * TOK, AD), f32),
        V((AK, ratio * TOK, AD), f32),
        V((AK, ratio * TOK, AD), f32),
        V((2, TOK, TOK), f32),
        V((near, 8, TOK), f32),
        V((n_row * n_dp, 8, TOK), f32),
        D((6, 2)),
        D((7, 2)),
        D((NG,)),
        D((NG,)),
        D((NG,)),
        D,
        D,
        D((NG,)),
        D((NG,)),
        D((near + n_row * n_dp,)),
        D((near + n_row * n_dp,)),
        D((7,)),
    ]
    mamba, attn, energy = pl.pallas_call(
        functools.partial(body, n_dp, n_ctx, near),
        out_shape=(
            pltpu.VMEM((TOK, H * P_SIZE), bf16),
            pltpu.VMEM((TOK, AQ * AD), bf16),
            jax.ShapeDtypeStruct((2, 2), f32),
        ),
        in_specs=specs,
        out_specs=(vmem, vmem, vmem),
        scratch_shapes=scratch,
        compiler_params=pltpu.CompilerParams(
            collective_id=0, has_side_effects=True, vmem_limit_bytes=60 * 1024 * 1024
        ),
        name="mixers",
    )(*operands)
    return mamba[None], attn[None], energy


def solution(mesh):
    placed = (
        P("dp", None),
        P("dp", None),
        P("dp", None),
        P("dp", "ctx", None),
        P("dp", None, "ctx"),
        P("dp", "ctx", None),
        P("dp", "ctx", None),
        P("dp", "ctx", None),
        P(),
        P(),
        P("dp", "ctx", None),
        P("dp", "ctx", None),
        P("dp", "ctx", None),
        P("dp", "ctx"),
    )
    n_dp, n_ctx = mesh.shape["dp"], mesh.shape["ctx"]
    return jax.shard_map(
        functools.partial(shards, n_dp, n_ctx, min(16, n_ctx)),
        mesh=mesh,
        in_specs=placed,
        out_specs=(P("dp", "ctx", None), P("dp", "ctx", None), P()),
        check_vma=False,
    )
```

```python
import functools
import math

import jax
import jax.numpy as jnp
from jax import lax
from jax.experimental import pallas as pl
from jax.experimental.pallas import tpu as pltpu
from jax.sharding import PartitionSpec as P

H = 64
P_SIZE = 64
N = 128
NG = 4
AQ = 32
AK = 8
AD = 128
HALF = 64
REACH = 3
TOK = 128
WIN = (2 * REACH + 1) * TOK
GW = (H // NG) * P_SIZE
HPG = H // NG

norm_eps = 1e-05
masked_score = -1e30
MESH = pl.DeviceIdType.MESH
HIGHEST = lax.Precision.HIGHEST
f32 = jnp.float32
bf16 = jnp.bfloat16
NT = (((1,), (1,)), ((), ()))
TN = (((0,), (0,)), ((), ()))
NN = (((1,), (0,)), ((), ()))


def dot(a, b, dims=NN, precision=None):
    return lax.dot_general(a, b, dims, precision=precision, preferred_element_type=f32)


def iota(shape, axis):
    return lax.broadcasted_iota(jnp.int32, shape, axis)


def body(
    n_dp,
    n_ctx,
    near,
    starts_ref,
    ends_ref,
    modes_ref,
    x_hbm,
    decay_ref,
    b_hbm,
    c_hbm,
    gate_hbm,
    skip_ref,
    gain_ref,
    q_hbm,
    k_hbm,
    v_hbm,
    lw_ref,
    mamba_ref,
    attn_ref,
    energy_ref,
    x_ref,
    b_ref,
    c_ref,
    gate_ref,
    q_ref,
    kbuf,
    vbuf,
    abuf,
    bbuf,
    hbuf,
    hsend,
    chead,
    wtail,
    reach,
    sbuf,
    ebuf,
    ewide,
    tbuf,
    tsend,
    fx,
    res,
    bias,
    mmask,
    lastm,
    carm,
    hot,
    runc,
    runr,
    acc,
    lsum,
    mtop,
    esq,
    e1,
    e2,
    kv_send,
    kv_recv,
    st_send,
    a_recv,
    b_recv,
    s_send,
    s_recv,
    rel1,
    h_send,
    h_recv,
    ch_send,
    ch_recv,
    en_send,
    en_recv,
    in_sem,
):
    b = lax.axis_index("ctx")
    dp = lax.axis_index("dp")
    core = b % 2
    row, lane_pos = b // near, b % near
    n_row = n_ctx // near
    seq = n_ctx * TOK
    first = b * TOK
    even, odd = core == 0, core == 1

    def peer(i):
        return {"ctx": i}

    barrier = pltpu.get_barrier_semaphore()

    def greet(device):
        pl.semaphore_signal(barrier, inc=1, device_id=device, device_id_type=MESH)

    columns = n_row * n_dp
    count = near - 1 + columns - 1
    for d in (-2, -1, 1, 2):
        ok = (b + d >= 0) & (b + d < n_ctx)

        @pl.when(ok)
        def _(d=d):
            greet({"ctx": b + d})

        count = count + jnp.where(ok, 1, 0)

    @pl.loop(1, near)
    def _(k):
        greet({"ctx": row * near + (lane_pos + k) % near})

    @pl.loop(1, columns)
    def _(k):
        i = (dp * n_row + row + k) % columns
        greet({"dp": i // n_row, "ctx": (i % n_row) * near + lane_pos})


    loads = [
        pltpu.make_async_copy(src, dst, in_sem.at[i])
        for i, (src, dst) in enumerate(
            (
                (x_hbm, x_ref),
                (b_hbm, b_ref),
                (c_hbm, c_ref),
                (k_hbm, kbuf.at[REACH]),
                (v_hbm, vbuf.at[REACH]),
                (q_hbm, q_ref),
                (gate_hbm, gate_ref),
            )
        )
    ]
    for load in loads:
        load.start()

    pl.semaphore_wait(barrier, count)

    def remote(src, dst, send, recv, to):
        return pltpu.make_async_remote_copy(
            src_ref=src,
            dst_ref=dst,
            send_sem=send,
            recv_sem=recv,
            device_id=peer(to),
            device_id_type=MESH,
        )

    def kv(which_send, from_slot, to_slot, to):
        k_src = k_hbm if from_slot is None else kbuf.at[from_slot]
        v_src = v_hbm if from_slot is None else vbuf.at[from_slot]
        return (
            remote(k_src, kbuf.at[to_slot], kv_send.at[which_send, 0], kv_recv.at[to_slot, 0], to),
            remote(v_src, vbuf.at[to_slot], kv_send.at[which_send, 1], kv_recv.at[to_slot, 1], to),
        )

    fwd2, bwd2 = b + 2 < n_ctx, b - 2 >= 0
    fwd1, bwd1 = b + 1 < n_ctx, b - 1 >= 0
    has_r2, has_l2 = bwd2, fwd2
    sends = [
        (fwd2, lambda: kv(0, None, 1, b + 2)),
        (bwd2, lambda: kv(1, None, 5, b - 2)),
        (even, lambda: kv(2, None, 2, b + 1)),
        (odd, lambda: kv(2, None, 4, b - 1)),
    ]
    relays = [
        (has_r2 & even, lambda: kv(3, 1, 0, b + 1)),
        (has_r2 & odd, lambda: kv(3, 1, 2, b - 1)),
        (has_l2 & even, lambda: kv(4, 5, 4, b + 1)),
        (has_l2 & odd, lambda: kv(4, 5, 6, b - 1)),
        (has_l2 & even & bwd1, lambda: kv(5, 5, 6, b - 1)),
    ]
    far = [(even & bwd1 & fwd2, lambda: kv(6, 2, 0, b + 2))]

    def start(plan):
        for when, make in plan:

            @pl.when(when)
            def _(make=make):
                for copy in make():
                    copy.start()

    def sent(plan):
        for when, make in plan:

            @pl.when(when)
            def _(make=make):
                for copy in make():
                    copy.wait_send()

    def arrived(slot):
        @pl.when((b - REACH + slot >= 0) & (b - REACH + slot < n_ctx))
        def _():
            for copy in kv(0, None, slot, b):
                copy.wait_recv()

    start(sends)

    def head_copy():
        return remote(c_hbm.at[:HALF], chead, ch_send, ch_recv, b - 2)

    @pl.when(even & bwd2)
    def _():
        head_copy().start()

    st_row = starts_ref[...].astype(f32)
    en_row = ends_ref[...].astype(f32)
    mo_row = modes_ref[...].astype(f32)
    docs = st_row.shape[1]
    diag = iota((docs, docs), 0) == iota((docs, docs), 1)

    def column(r):
        return jnp.sum(jnp.where(diag, r, 0.0), axis=1, keepdims=True)

    st_col, en_col, mo_col = column(st_row), column(en_row), column(mo_row)
    first_f = first.astype(f32)
    pos_col = first_f + iota((TOK, 1), 0).astype(f32)
    below = st_row <= pos_col
    member = jnp.where(below & (pos_col < en_row), 1.0, 0.0)
    cnt_col = jnp.sum(jnp.where(below, 1.0, 0.0), axis=1, keepdims=True)
    begin_col = jnp.sum(member * st_row, axis=1, keepdims=True)
    mode_col = jnp.sum(member * mo_row, axis=1, keepdims=True)
    key_pos = first_f - float(REACH * TOK) + iota((1, WIN), 1).astype(f32)
    cnt_row = jnp.sum(jnp.where(st_col <= key_pos, 1.0, 0.0), axis=0, keepdims=True)
    present = (key_pos >= 0.0) & (key_pos < float(seq))
    same = (cnt_row == cnt_col) & present
    allowed = same & ((key_pos <= pos_col) | (mode_col == 1.0))
    bias[...] = jnp.where(allowed, 0.0, masked_score)
    own = slice(REACH * TOK, (REACH + 1) * TOK)
    own_same = cnt_row[:, own] == cnt_col
    mmask[...] = jnp.where(own_same & (iota((TOK, TOK), 1) <= iota((TOK, TOK), 0)), 1.0, 0.0)
    lastm[...] = jnp.broadcast_to(
        jnp.where(cnt_col == cnt_col[TOK - 1 :, :], 1.0, 0.0), (TOK, TOK)
    )
    carried = jnp.where(begin_col < first_f, 1.0, 0.0)
    carm[...] = jnp.broadcast_to(carried, (TOK, TOK))

    def goes_on(base):
        end = jnp.where((st_row < base) & (base <= en_row), en_row, 0.0)
        return jnp.sum(jnp.where(end > base + float(2 * TOK + HALF), 1.0, 0.0), axis=1, keepdims=True)

    chip_first = (first - core * TOK).astype(f32)
    rows_out = goes_on(first_f + float(TOK))
    rows_in = goes_on(chip_first)
    rows_before = goes_on(chip_first - float(2 * TOK))
    own_pos = key_pos[:, own]
    own_member = jnp.where((st_col <= own_pos) & (own_pos < en_col), 1.0, 0.0)
    mode_row = jnp.sum(own_member * mo_col, axis=0, keepdims=True)
    which = iota((8, TOK), 0).astype(f32)
    hot[...] = jnp.where(which == mode_row, lw_ref[...], 0.0)

    upto = jnp.where(iota((TOK, TOK), 0) >= iota((TOK, TOK), 1), 1.0, 0.0)
    decay = decay_ref[...]
    runr[...] = dot(decay, upto, NT, HIGHEST)
    for g in range(NG):
        runc[g, :, :HPG] = dot(upto, decay[g * HPG : (g + 1) * HPG, :], NT, HIGHEST)
    esq[...] = jnp.zeros_like(esq)

    for i in (0, 1, 2, 4, 5, 6):

        @pl.when((b - REACH + i < 0) | (b - REACH + i >= n_ctx))
        def _(i=i):
            kbuf[i] = jnp.zeros((TOK, AK * AD), bf16)
            vbuf[i] = jnp.zeros((TOK, AK * AD), bf16)

    @pl.when(b == 0)
    def _():
        abuf[...] = jnp.zeros_like(abuf)
        sbuf[...] = jnp.zeros_like(sbuf)

    @pl.when(b < 4)
    def _():
        hbuf[...] = jnp.zeros_like(hbuf)

    @pl.when(b < 3)
    def _():
        bbuf[...] = jnp.zeros_like(bbuf)

    for load in loads[:3]:
        load.wait()

    lane = iota((TOK, TOK), 1)
    left = lane < P_SIZE

    def state_copy(g):
        return remote(ebuf.at[g], abuf.at[g], st_send.at[g], a_recv.at[g], b + 1)

    def scale_copy():
        return remote(tsend, sbuf, s_send, s_recv, b + 1)

    @pl.loop(0, NG)
    def _(g):
        cols = runc[g]
        parts = []
        for pair in range(HPG // 2):
            at = slice(pair * TOK, (pair + 1) * TOK)
            c0 = jnp.broadcast_to(cols[:, 2 * pair : 2 * pair + 1], (TOK, TOK))
            c1 = jnp.broadcast_to(cols[:, 2 * pair + 1 : 2 * pair + 2], (TOK, TOK))
            both = jnp.where(left, c0, c1)
            end = both[TOK - 1 :, :]
            fx[g, :, at] = jnp.exp(both) * carm[...]
            tbuf[g, :, at] = jnp.exp(end) * carm[TOK - 1 :, :]
            tail = jnp.exp(end - both) * lastm[...]
            lanes = pl.ds(pl.multiple_of(g * GW + pair * TOK, TOK), TOK)
            parts.append((x_ref[:, lanes].astype(f32) * tail).astype(bf16))
        weighted = jnp.concatenate(parts, axis=1)
        wtail[g] = weighted[HALF:, :]
        b_grp = b_ref[:, pl.ds(pl.multiple_of(g * N, N), N)]
        e = dot(b_grp, weighted, TN)
        ewide[g] = e
        ebuf[g] = e.astype(bf16)

        @pl.when(even)
        def _():
            state_copy(g).start()

    @pl.when(even)
    def _():
        tsend[...] = tbuf[...]
        scale_copy().start()

    @pl.when(odd)
    def _():
        scale_copy().wait_recv()
        tsend[...] = tbuf[...] * sbuf[...]

        @pl.when(fwd1)
        def _():
            scale_copy().start()

    def combine(g):
        state_copy(g).wait_recv()
        state = ewide[g] + tbuf[g] * abuf[g].astype(f32)
        top = wtail[g].astype(f32)
        b_rows = b_ref[HALF:, g * N : (g + 1) * N].astype(f32)
        low = jnp.concatenate([b_rows, top[:, N:]], axis=1)
        rows = jnp.concatenate([top, low], axis=0)
        ebuf[g] = jnp.where(rows_out > 0.5, rows, state).astype(bf16)

        @pl.when(fwd1)
        def _():
            state_copy(g).start()

    @pl.when(odd)
    def _():
        for g in range(NG):
            combine(g)

    @pl.loop(0, NG)
    def _(g):
        lanes_n = pl.ds(pl.multiple_of(g * N, N), N)
        both_docs = dot(c_ref[:, lanes_n], b_ref[:, lanes_n], NT) * mmask[...]
        cols = runc[g]
        rows = runr[pl.ds(pl.multiple_of(g * HPG, HPG), HPG), :]
        for pair in range(HPG // 2):
            at = slice(pair * TOK, (pair + 1) * TOK)
            mixes = []
            for h in (2 * pair, 2 * pair + 1):
                spread = cols[:, h : h + 1] - rows[h : h + 1, :]
                mixes.append((jnp.exp(jnp.minimum(spread, 0.0)) * both_docs).astype(bf16))
            xp = x_ref[:, pl.ds(pl.multiple_of(g * GW + pair * TOK, TOK), TOK)]
            zero = jnp.zeros_like(xp)
            split = jnp.concatenate([jnp.where(left, xp, zero), jnp.where(left, zero, xp)], axis=0)
            inner = dot(jnp.concatenate(mixes, axis=1), split)
            h0 = g * HPG + 2 * pair
            skip = jnp.where(left, skip_ref[h0], skip_ref[h0 + 1])
            res[g, :, at] = inner + skip * xp.astype(f32)

    arrived(1)
    arrived(5)
    start(relays)
    ratio = AQ // AK
    scale = AD ** (-0.5) * math.log2(math.e)

    def attend(j, slots):
        heads = pl.ds(pl.multiple_of(j * AD, AD), AD)
        q = jnp.concatenate(
            [
                q_ref[:, pl.ds(pl.multiple_of(j * ratio * AD + r * AD, AD), AD)]
                for r in range(ratio)
            ],
            axis=0,
        )
        keys = jnp.concatenate(
            [kbuf[i, :, heads] for i in slots], axis=0
        )
        values = jnp.concatenate(
            [vbuf[i, :, heads] for i in slots], axis=0
        )
        masks = jnp.concatenate([bias[:, i * TOK : (i + 1) * TOK] for i in slots], axis=1)
        s = dot(q, keys, NT) * scale
        s = s.reshape(ratio, TOK, len(slots) * TOK) + masks[None]
        s = s.reshape(ratio * TOK, len(slots) * TOK)
        wide = jnp.concatenate([values, jnp.ones_like(values)], axis=1)
        return s, wide

    for load in loads[3:]:
        load.wait()
    near_slots, far_slots = (1, 2, 3, 4, 5), (0, 6)
    arrived(2)
    start(far)
    arrived(4)

    def relay_state(g):
        up = remote(abuf.at[g], bbuf.at[g], rel1.at[g], b_recv.at[g], b + 1)
        over = remote(hsend.at[g], hbuf.at[g], h_send.at[g], h_recv.at[g], b + 2)
        return up, over

    def pass_on(g):
        @pl.when(even & bwd1)
        def _():
            state_copy(g).wait_recv()
            up, over = relay_state(g)

            up.start()

            @pl.when(fwd2)
            def _():
                raw = abuf[g]
                c_rows = chead[:, pl.ds(pl.multiple_of(g * N, N), N)]
                seen = dot(c_rows, raw)
                kept = jnp.where(rows_in > 0.5, raw[:HALF].astype(f32), seen)
                hsend[g, :, :GW] = kept.astype(bf16)
                hsend[g, :, GW:] = raw[HALF:, :N]
                over.start()

    @pl.when(even & fwd2)
    def _():
        remote(chead, chead, ch_send, ch_recv, b).wait_recv()

    @pl.loop(0, NG)
    def _(g):
        for half in range(AK // NG):
            j = g * (AK // NG) + half
            s, wide = attend(j, near_slots)
            top = jnp.max(s, axis=1, keepdims=True)
            p = jnp.exp2(s - top).astype(bf16)
            o = dot(p, wide)
            acc[j] = o[:, :AD]
            lsum[j] = o[:, AD:]
            mtop[j] = jnp.broadcast_to(top, (ratio * TOK, AD))
        pass_on(g)

    arrived(0)
    arrived(6)

    @pl.loop(0, AK)
    def _(j):
        s, wide = attend(j, far_slots)
        before = mtop[j]
        top = jnp.maximum(before, jnp.max(s, axis=1, keepdims=True))
        p = jnp.exp2(s - jnp.concatenate([top] * len(far_slots), axis=1)).astype(bf16)
        o = dot(p, wide)
        fade = jnp.exp2(before - top)
        total = lsum[j] * fade + o[:, AD:]
        out = ((acc[j] * fade + o[:, :AD]) / total).astype(bf16)
        square = jnp.zeros((TOK, AD), f32)
        for r in range(ratio):
            piece = out[r * TOK : (r + 1) * TOK]
            attn_ref[:, pl.ds(pl.multiple_of(j * ratio * AD + r * AD, AD), AD)] = piece
            wide_piece = piece.astype(f32)
            square = square + wide_piece * wide_piece
        esq[1] = esq[1] + square

    @pl.when(even & bwd1)
    def _():
        scale_copy().wait_recv()

    def unpack(raw):
        built = dot(raw[HALF:, :N], raw[:HALF, :], TN)
        return jnp.where(rows_in > 0.5, built, raw.astype(f32)).astype(bf16)

    @pl.loop(0, NG)
    def _(g):
        c_grp = c_ref[:, pl.ds(pl.multiple_of(g * N, N), N)]

        @pl.when(even)
        def _():
            near_part = dot(c_grp, unpack(abuf[g]))

            @pl.when(b >= 4)
            def _():
                remote(hbuf.at[g], hbuf.at[g], h_send.at[g], h_recv.at[g], b).wait_recv()

            half = hbuf[g, :, :GW]
            built = dot(hbuf[g, :, GW:], half, TN).astype(bf16)
            seen = half.astype(f32)
            seen = jnp.concatenate([seen, jnp.zeros_like(seen)], axis=0)
            far_part = jnp.where(rows_before > 0.5, dot(c_grp, built), seen)
            reach[...] = near_part + far_part * sbuf[g]

        @pl.when(odd)
        def _():
            near_part = dot(c_grp, abuf[g])

            @pl.when(b >= 3)
            def _():
                remote(bbuf.at[g], bbuf.at[g], rel1.at[g], b_recv.at[g], b).wait_recv()

            reach[...] = near_part + dot(c_grp, unpack(bbuf[g])) * sbuf[g]

        reached = reach[...]
        lanes = pl.ds(pl.multiple_of(g * GW, GW), GW)
        result = res[g] + reached * fx[g]
        z = gate_ref[:, lanes].astype(f32)
        gated = result * (z / (1.0 + jnp.exp(-z)))
        square = jnp.sum(gated * gated, axis=1, keepdims=True) * (1.0 / GW)
        mixed = (gated * lax.rsqrt(square + norm_eps) * gain_ref[:, lanes]).astype(bf16)
        mamba_ref[:, lanes] = mixed
        again = mixed.astype(f32)
        again = again * again
        part = again[:, :TOK]
        for i in range(1, GW // TOK):
            part = part + again[:, i * TOK : (i + 1) * TOK]
        esq[0] = esq[0] + part

    per_mode = [
        jnp.sum(dot(hot[...], esq[i], NN, HIGHEST), axis=1, keepdims=True) for i in range(2)
    ]
    small = iota((8, TOK), 1)
    denom = float(n_dp * n_ctx * TOK) * float(H * P_SIZE)
    mine = jnp.where(small == 0, per_mode[0], jnp.where(small == 1, per_mode[1], 0.0)) / denom

    def exchange(buf, size, me, base, device_of, value):
        buf[me] = value

        def copy(to_index, from_index):
            return pltpu.make_async_remote_copy(
                src_ref=buf.at[me],
                dst_ref=buf.at[from_index],
                send_sem=en_send.at[base + to_index],
                recv_sem=en_recv.at[base + from_index],
                device_id=device_of(to_index),
                device_id_type=MESH,
            )

        for k in sorted(range(1, size), key=lambda k: -min(k, size - k)):
            copy((me + k) % size, me).start()

        @pl.loop(1, size)
        def _(k):
            other = (me + k) % size
            copy(other, other).wait_recv()

        total = buf[0]
        for i in range(1, size):
            total = total + buf[i]
        return total, lambda k: copy((me + k) % size, me).wait_send()

    done = []
    value = mine
    plans = (
        (e1, near, lane_pos, 0, lambda i: {"ctx": row * near + i}),
        (
            e2,
            n_row * n_dp,
            dp * n_row + row,
            near,
            lambda i: {"dp": i // n_row, "ctx": (i % n_row) * near + lane_pos},
        ),
    )
    for buf, size, me, base, device_of in plans:
        if size > 1:
            value, wait = exchange(buf, size, me, base, device_of, value)
            done.append((size, wait))
    energy_ref[...] = value[:2, :2]

    for size, wait in done:

        @pl.loop(1, size)
        def _(k, wait=wait):
            wait(k)

    sent(sends)
    sent(relays)
    sent(far)

    @pl.when(even | fwd1)
    def _():
        scale_copy().wait_send()

        @pl.loop(0, NG)
        def _(g):
            state_copy(g).wait_send()

    @pl.when(even & bwd2)
    def _():
        head_copy().wait_send()

    @pl.when(even & bwd1)
    def _():
        @pl.loop(0, NG)
        def _(g):
            up, over = relay_state(g)
            up.wait_send()

            @pl.when(fwd2)
            def _():
                over.wait_send()


def put_out(*refs):
    sem = refs[-1]
    copies = [pltpu.make_async_copy(refs[i], refs[3 + i], sem.at[i]) for i in range(3)]
    for copy in copies:
        copy.start()
    for copy in copies:
        copy.wait()


def shards(n_dp, n_ctx, near, *args):
    (starts, ends, modes, x, decay, b_in, c_in, gate, skip, gain, q, k, v, lw) = args
    operands = (
        starts,
        ends,
        modes,
        x[0],
        decay[0],
        b_in[0],
        c_in[0],
        gate[0],
        skip,
        gain.reshape(1, H * P_SIZE),
        q[0],
        k[0],
        v[0],
        lw,
    )
    vmem = pl.BlockSpec(memory_space=pltpu.VMEM)
    smem = pl.BlockSpec(memory_space=pltpu.SMEM)
    hbm = pl.BlockSpec(memory_space=pl.ANY)
    specs = [vmem] * 3 + [hbm, vmem, hbm, hbm, hbm, smem, vmem, hbm, hbm, hbm, vmem]
    n_row = n_ctx // near
    V, D = pltpu.VMEM, pltpu.SemaphoreType.DMA
    ratio = AQ // AK
    scratch = [
        V((TOK, H * P_SIZE), bf16),
        V((TOK, NG * N), bf16),
        V((TOK, NG * N), bf16),
        V((TOK, H * P_SIZE), bf16),
        V((TOK, AQ * AD), bf16),
        V((2 * REACH + 1, TOK, AK * AD), bf16),
        V((2 * REACH + 1, TOK, AK * AD), bf16),
        V((NG, N, GW), bf16),
        V((NG, N, GW), bf16),
        V((NG, HALF, GW + N), bf16),
        V((NG, HALF, GW + N), bf16),
        V((HALF, NG * N), bf16),
        V((NG, HALF, GW), bf16),
        V((TOK, GW), f32),
        V((NG, 1, GW), f32),
        V((NG, N, GW), bf16),
        V((NG, N, GW), f32),
        V((NG, 1, GW), f32),
        V((NG, 1, GW), f32),
        V((NG, TOK, GW), f32),
        V((NG, TOK, GW), f32),
        V((TOK, WIN), f32),
        V((TOK, TOK), f32),
        V((TOK, TOK), f32),
        V((TOK, TOK), f32),
        V((8, TOK), f32),
        V((NG, TOK, TOK), f32),
        V((H, TOK), f32),
        V((AK, ratio * TOK, AD), f32),
        V((AK, ratio * TOK, AD), f32),
        V((AK, ratio * TOK, AD), f32),
        V((2, TOK, TOK), f32),
        V((near, 8, TOK), f32),
        V((n_row * n_dp, 8, TOK), f32),
        D((7, 2)),
        D((7, 2)),
        D((NG,)),
        D((NG,)),
        D((NG,)),
        D,
        D,
        D((NG,)),
        D((NG,)),
        D((NG,)),
        D,
        D,
        D((near + n_row * n_dp,)),
        D((near + n_row * n_dp,)),
        D((7,)),
    ]
    mamba, attn, energy = pl.pallas_call(
        functools.partial(body, n_dp, n_ctx, near),
        out_shape=(
            pltpu.VMEM((TOK, H * P_SIZE), bf16),
            pltpu.VMEM((TOK, AQ * AD), bf16),
            pltpu.VMEM((2, 2), f32),
        ),
        in_specs=specs,
        out_specs=(vmem, vmem, vmem),
        scratch_shapes=scratch,
        compiler_params=pltpu.CompilerParams(
            collective_id=0, has_side_effects=True, vmem_limit_bytes=60 * 1024 * 1024
        ),
        name="mixers",
    )(*operands)
    results = (mamba, attn, energy)
    mamba, attn, energy = pl.pallas_call(
        put_out,
        out_shape=tuple(jax.ShapeDtypeStruct(r.shape, r.dtype) for r in results),
        in_specs=[vmem] * 3,
        out_specs=(hbm,) * 3,
        scratch_shapes=[D((3,))],
        name="put_out",
    )(*[pltpu.with_memory_space_constraint(r, pltpu.VMEM) for r in results])
    return mamba[None], attn[None], energy


def solution(mesh):
    placed = (
        P("dp", None),
        P("dp", None),
        P("dp", None),
        P("dp", "ctx", None),
        P("dp", None, "ctx"),
        P("dp", "ctx", None),
        P("dp", "ctx", None),
        P("dp", "ctx", None),
        P(),
        P(),
        P("dp", "ctx", None),
        P("dp", "ctx", None),
        P("dp", "ctx", None),
        P("dp", "ctx"),
    )
    n_dp, n_ctx = mesh.shape["dp"], mesh.shape["ctx"]
    return jax.shard_map(
        functools.partial(shards, n_dp, n_ctx, min(16, n_ctx)),
        mesh=mesh,
        in_specs=placed,
        out_specs=(P("dp", "ctx", None), P("dp", "ctx", None), P()),
        check_vma=False,
    )
```

```python
import functools
import math

import jax
import jax.numpy as jnp
from jax import lax
from jax.experimental import pallas as pl
from jax.experimental.pallas import tpu as pltpu
from jax.sharding import PartitionSpec as P

H = 64
P_SIZE = 64
N = 128
NG = 4
AQ = 32
AK = 8
AD = 128
HALF = 64
REACH = 3
TOK = 128
WIN = (2 * REACH + 1) * TOK
GW = (H // NG) * P_SIZE
HPG = H // NG

norm_eps = 1e-05
masked_score = -1e30
MESH = pl.DeviceIdType.MESH
HIGHEST = lax.Precision.HIGHEST
f32 = jnp.float32
bf16 = jnp.bfloat16
NT = (((1,), (1,)), ((), ()))
TN = (((0,), (0,)), ((), ()))
NN = (((1,), (0,)), ((), ()))


def dot(a, b, dims=NN, precision=None):
    return lax.dot_general(a, b, dims, precision=precision, preferred_element_type=f32)


def iota(shape, axis):
    return lax.broadcasted_iota(jnp.int32, shape, axis)


def body(
    n_dp,
    n_ctx,
    near,
    starts_ref,
    ends_ref,
    modes_ref,
    x_hbm,
    decay_ref,
    b_hbm,
    c_hbm,
    gate_hbm,
    skip_ref,
    gain_ref,
    q_hbm,
    k_hbm,
    v_hbm,
    lw_ref,
    mamba_ref,
    attn_ref,
    energy_ref,
    x_ref,
    b_ref,
    c_ref,
    gate_ref,
    q_ref,
    kbuf,
    vbuf,
    abuf,
    bbuf,
    hbuf,
    hsend,
    chead,
    wtail,
    reach,
    lift,
    sbuf,
    ebuf,
    ewide,
    tbuf,
    tsend,
    fx,
    res,
    bias,
    mmask,
    lastm,
    carm,
    hot,
    runc,
    runr,
    acc,
    lsum,
    mtop,
    esq,
    e1,
    e2,
    kv_send,
    kv_recv,
    st_send,
    a_recv,
    b_recv,
    s_send,
    s_recv,
    rel1,
    h_send,
    h_recv,
    ch_send,
    chn_send,
    ch_recv,
    en_send,
    en_recv,
    in_sem,
):
    b = lax.axis_index("ctx")
    dp = lax.axis_index("dp")
    core = b % 2
    row, lane_pos = b // near, b % near
    n_row = n_ctx // near
    seq = n_ctx * TOK
    first = b * TOK
    even, odd = core == 0, core == 1

    def peer(i):
        return {"ctx": i}

    barrier = pltpu.get_barrier_semaphore()

    def greet(device):
        pl.semaphore_signal(barrier, inc=1, device_id=device, device_id_type=MESH)

    columns = n_row * n_dp
    count = near - 1 + columns - 1
    for d in (-2, -1, 1, 2):
        ok = (b + d >= 0) & (b + d < n_ctx)

        @pl.when(ok)
        def _(d=d):
            greet({"ctx": b + d})

        count = count + jnp.where(ok, 1, 0)

    @pl.loop(1, near)
    def _(k):
        greet({"ctx": row * near + (lane_pos + k) % near})

    @pl.loop(1, columns)
    def _(k):
        i = (dp * n_row + row + k) % columns
        greet({"dp": i // n_row, "ctx": (i % n_row) * near + lane_pos})


    loads = [
        pltpu.make_async_copy(src, dst, in_sem.at[i])
        for i, (src, dst) in enumerate(
            (
                (x_hbm, x_ref),
                (b_hbm, b_ref),
                (c_hbm, c_ref),
                (k_hbm, kbuf.at[REACH]),
                (v_hbm, vbuf.at[REACH]),
                (q_hbm, q_ref),
                (gate_hbm, gate_ref),
            )
        )
    ]
    for load in loads:
        load.start()

    pl.semaphore_wait(barrier, count)

    def remote(src, dst, send, recv, to):
        return pltpu.make_async_remote_copy(
            src_ref=src,
            dst_ref=dst,
            send_sem=send,
            recv_sem=recv,
            device_id=peer(to),
            device_id_type=MESH,
        )

    def kv(which_send, from_slot, to_slot, to):
        k_src = k_hbm if from_slot is None else kbuf.at[from_slot]
        v_src = v_hbm if from_slot is None else vbuf.at[from_slot]
        return (
            remote(k_src, kbuf.at[to_slot], kv_send.at[which_send, 0], kv_recv.at[to_slot, 0], to),
            remote(v_src, vbuf.at[to_slot], kv_send.at[which_send, 1], kv_recv.at[to_slot, 1], to),
        )

    fwd2, bwd2 = b + 2 < n_ctx, b - 2 >= 0
    fwd1, bwd1 = b + 1 < n_ctx, b - 1 >= 0
    has_r2, has_l2 = bwd2, fwd2
    sends = [
        (fwd2, lambda: kv(0, None, 1, b + 2)),
        (bwd2, lambda: kv(1, None, 5, b - 2)),
        (even, lambda: kv(2, None, 2, b + 1)),
        (odd, lambda: kv(2, None, 4, b - 1)),
    ]
    relays = [
        (has_r2 & even, lambda: kv(3, 1, 0, b + 1)),
        (has_r2 & odd, lambda: kv(3, 1, 2, b - 1)),
        (has_l2 & even, lambda: kv(4, 5, 4, b + 1)),
        (has_l2 & odd, lambda: kv(4, 5, 6, b - 1)),
        (has_l2 & even & bwd1, lambda: kv(5, 5, 6, b - 1)),
    ]

    def half_kv(to):
        return tuple(
            remote(buf.at[2, HALF:], buf.at[0, HALF:], kv_send.at[6, i], kv_recv.at[0, i], to)
            for i, buf in enumerate((kbuf, vbuf))
        )

    far = [(even & bwd1 & fwd2, lambda: half_kv(b + 2))]

    def start(plan):
        for when, make in plan:

            @pl.when(when)
            def _(make=make):
                for copy in make():
                    copy.start()

    def sent(plan):
        for when, make in plan:

            @pl.when(when)
            def _(make=make):
                for copy in make():
                    copy.wait_send()

    def arrived(slot):
        @pl.when((b - REACH + slot >= 0) & (b - REACH + slot < n_ctx))
        def _():
            for copy in kv(0, None, slot, b):
                copy.wait_recv()

    start(sends)

    def head_copy():
        return remote(c_hbm.at[:HALF], chead, ch_send, ch_recv, b - 2)

    def near_head_copy():
        return remote(c_hbm.at[:HALF], chead, chn_send, ch_recv, b - 1)

    @pl.when(even & bwd2)
    def _():
        near_head_copy().start()
        head_copy().start()

    st_row = starts_ref[...].astype(f32)
    en_row = ends_ref[...].astype(f32)
    mo_row = modes_ref[...].astype(f32)
    docs = st_row.shape[1]
    diag = iota((docs, docs), 0) == iota((docs, docs), 1)

    def column(r):
        return jnp.sum(jnp.where(diag, r, 0.0), axis=1, keepdims=True)

    st_col, en_col, mo_col = column(st_row), column(en_row), column(mo_row)
    first_f = first.astype(f32)
    pos_col = first_f + iota((TOK, 1), 0).astype(f32)
    below = st_row <= pos_col
    member = jnp.where(below & (pos_col < en_row), 1.0, 0.0)
    cnt_col = jnp.sum(jnp.where(below, 1.0, 0.0), axis=1, keepdims=True)
    begin_col = jnp.sum(member * st_row, axis=1, keepdims=True)
    mode_col = jnp.sum(member * mo_row, axis=1, keepdims=True)
    key_pos = first_f - float(REACH * TOK) + iota((1, WIN), 1).astype(f32)
    cnt_row = jnp.sum(jnp.where(st_col <= key_pos, 1.0, 0.0), axis=0, keepdims=True)
    present = (key_pos >= 0.0) & (key_pos < float(seq))
    same = (cnt_row == cnt_col) & present
    allowed = same & ((key_pos <= pos_col) | (mode_col == 1.0))
    bias[...] = jnp.where(allowed, 0.0, masked_score)
    own = slice(REACH * TOK, (REACH + 1) * TOK)
    own_same = cnt_row[:, own] == cnt_col
    mmask[...] = jnp.where(own_same & (iota((TOK, TOK), 1) <= iota((TOK, TOK), 0)), 1.0, 0.0)
    lastm[...] = jnp.broadcast_to(
        jnp.where(cnt_col == cnt_col[TOK - 1 :, :], 1.0, 0.0), (TOK, TOK)
    )
    carried = jnp.where(begin_col < first_f, 1.0, 0.0)
    carm[...] = jnp.broadcast_to(carried, (TOK, TOK))

    def goes_on(base):
        end = jnp.where((st_row < base) & (base <= en_row), en_row, 0.0)
        return jnp.sum(jnp.where(end > base + float(2 * TOK + HALF), 1.0, 0.0), axis=1, keepdims=True)

    def ends_soon(base):
        end = jnp.where((st_row < base) & (base <= en_row), en_row, 0.0)
        return jnp.sum(end, axis=1, keepdims=True) <= base + float(HALF)

    chip_first = (first - core * TOK).astype(f32)
    short_out = jnp.where(ends_soon(first_f + float(TOK)), 1.0, 0.0)
    short_in = jnp.where(ends_soon(chip_first), 1.0, 0.0)
    rows_out = goes_on(first_f + float(TOK))
    rows_in = goes_on(chip_first)
    rows_before = goes_on(chip_first - float(2 * TOK))
    own_pos = key_pos[:, own]
    own_member = jnp.where((st_col <= own_pos) & (own_pos < en_col), 1.0, 0.0)
    mode_row = jnp.sum(own_member * mo_col, axis=0, keepdims=True)
    which = iota((8, TOK), 0).astype(f32)
    hot[...] = jnp.where(which == mode_row, lw_ref[...], 0.0)

    upto = jnp.where(iota((TOK, TOK), 0) >= iota((TOK, TOK), 1), 1.0, 0.0)
    decay = decay_ref[...]
    runr[...] = dot(decay, upto, NT, HIGHEST)
    for g in range(NG):
        runc[g, :, :HPG] = dot(upto, decay[g * HPG : (g + 1) * HPG, :], NT, HIGHEST)
    esq[...] = jnp.zeros_like(esq)

    for i in (0, 1, 2, 4, 5, 6):

        @pl.when((b - REACH + i < 0) | (b - REACH + i >= n_ctx))
        def _(i=i):
            kbuf[i] = jnp.zeros((TOK, AK * AD), bf16)
            vbuf[i] = jnp.zeros((TOK, AK * AD), bf16)

    @pl.when(b == 0)
    def _():
        abuf[...] = jnp.zeros_like(abuf)
        sbuf[...] = jnp.zeros_like(sbuf)

    @pl.when(b < 4)
    def _():
        hbuf[...] = jnp.zeros_like(hbuf)

    @pl.when(b < 3)
    def _():
        bbuf[...] = jnp.zeros_like(bbuf)

    for load in loads[:3]:
        load.wait()

    lane = iota((TOK, TOK), 1)
    left = lane < P_SIZE

    def state_copy(g):
        return remote(ebuf.at[g], abuf.at[g], st_send.at[g], a_recv.at[g], b + 1)

    def scale_copy():
        return remote(tsend, sbuf, s_send, s_recv, b + 1)

    @pl.loop(0, NG)
    def _(g):
        cols = runc[g]
        parts = []
        for pair in range(HPG // 2):
            at = slice(pair * TOK, (pair + 1) * TOK)
            c0 = jnp.broadcast_to(cols[:, 2 * pair : 2 * pair + 1], (TOK, TOK))
            c1 = jnp.broadcast_to(cols[:, 2 * pair + 1 : 2 * pair + 2], (TOK, TOK))
            both = jnp.where(left, c0, c1)
            end = both[TOK - 1 :, :]
            fx[g, :, at] = jnp.exp(both) * carm[...]
            tbuf[g, :, at] = jnp.exp(end) * carm[TOK - 1 :, :]
            tail = jnp.exp(end - both) * lastm[...]
            lanes = pl.ds(pl.multiple_of(g * GW + pair * TOK, TOK), TOK)
            parts.append((x_ref[:, lanes].astype(f32) * tail).astype(bf16))
        weighted = jnp.concatenate(parts, axis=1)
        wtail[g] = weighted[HALF:, :]
        b_grp = b_ref[:, pl.ds(pl.multiple_of(g * N, N), N)]
        e = dot(b_grp, weighted, TN)
        ewide[g] = e
        ebuf[g] = e.astype(bf16)

        @pl.when(even)
        def _():
            state_copy(g).start()

    @pl.when(even)
    def _():
        tsend[...] = tbuf[...]
        scale_copy().start()

    @pl.when(odd)
    def _():
        scale_copy().wait_recv()
        tsend[...] = tbuf[...] * sbuf[...]

        @pl.when(fwd1)
        def _():
            scale_copy().start()

    def combine(g):
        state_copy(g).wait_recv()
        state = ewide[g] + tbuf[g] * abuf[g].astype(f32)
        top = wtail[g].astype(f32)
        b_rows = b_ref[HALF:, g * N : (g + 1) * N].astype(f32)
        low = jnp.concatenate([b_rows, top[:, N:]], axis=1)
        rows = jnp.concatenate([top, low], axis=0)
        kept = jnp.where(rows_out > 0.5, rows, state)
        seen = dot(chead[:, g * N : (g + 1) * N], state.astype(bf16))
        if g == NG - 2:
            low = kbuf[1, :HALF, :].astype(f32)
        if g == NG - 1:
            low = vbuf[1, :HALF, :].astype(f32)
        brief = jnp.concatenate([seen, low], axis=0)
        ebuf[g] = jnp.where(short_out > 0.5, brief, kept).astype(bf16)

        @pl.when(fwd1)
        def _():
            state_copy(g).start()

    @pl.when(odd)
    def _():
        @pl.when(fwd1)
        def _():
            remote(chead, chead, ch_send, ch_recv, b).wait_recv()

        @pl.when(b == n_ctx - 1)
        def _():
            chead[...] = jnp.zeros_like(chead)

        for g in range(NG - 2):
            combine(g)

    for load in loads[3:]:
        load.wait()

    @pl.loop(0, NG)
    def _(g):
        z = gate_ref[:, pl.ds(pl.multiple_of(g * GW, GW), GW)].astype(f32)
        lift[g] = z / (1.0 + jnp.exp(-z))
        lanes_n = pl.ds(pl.multiple_of(g * N, N), N)
        both_docs = dot(c_ref[:, lanes_n], b_ref[:, lanes_n], NT) * mmask[...]
        cols = runc[g]
        rows = runr[pl.ds(pl.multiple_of(g * HPG, HPG), HPG), :]
        for pair in range(HPG // 2):
            at = slice(pair * TOK, (pair + 1) * TOK)
            mixes = []
            for h in (2 * pair, 2 * pair + 1):
                spread = cols[:, h : h + 1] - rows[h : h + 1, :]
                mixes.append((jnp.exp(jnp.minimum(spread, 0.0)) * both_docs).astype(bf16))
            xp = x_ref[:, pl.ds(pl.multiple_of(g * GW + pair * TOK, TOK), TOK)]
            zero = jnp.zeros_like(xp)
            split = jnp.concatenate([jnp.where(left, xp, zero), jnp.where(left, zero, xp)], axis=0)
            inner = dot(jnp.concatenate(mixes, axis=1), split)
            h0 = g * HPG + 2 * pair
            skip = jnp.where(left, skip_ref[h0], skip_ref[h0 + 1])
            res[g, :, at] = inner + skip * xp.astype(f32)


    ratio = AQ // AK
    scale = AD ** (-0.5) * math.log2(math.e)

    def block_lanes(i):
        if isinstance(i, int):
            return slice(i * TOK, (i + 1) * TOK)
        return pl.ds(pl.multiple_of(i * TOK, TOK), TOK)

    def attend(j, slots):
        heads = pl.ds(pl.multiple_of(j * AD, AD), AD)
        q = jnp.concatenate(
            [
                q_ref[:, pl.ds(pl.multiple_of(j * ratio * AD + r * AD, AD), AD)]
                for r in range(ratio)
            ],
            axis=0,
        )
        keys = jnp.concatenate(
            [kbuf[i, :, heads] for i in slots], axis=0
        )
        values = jnp.concatenate(
            [vbuf[i, :, heads] for i in slots], axis=0
        )
        masks = jnp.concatenate([bias[:, block_lanes(i)] for i in slots], axis=1)
        s = dot(q, keys, NT) * scale
        s = s.reshape(ratio, TOK, len(slots) * TOK) + masks[None]
        s = s.reshape(ratio * TOK, len(slots) * TOK)
        wide = jnp.concatenate([values, jnp.ones_like(values)], axis=1)
        return s, wide

    beside = jnp.where(even, REACH + 1, REACH - 1)
    chip_slots = (REACH, beside)
    far_one = jnp.where(even, 0, 2 * REACH)
    near_slots = (1, 5, 2 * REACH - beside, 2 * REACH - far_one)
    far_slots = (far_one,)

    @pl.when(even)
    def _():
        arrived(4)

    @pl.when(odd)
    def _():
        arrived(2)

    @pl.loop(0, AK)
    def _(j):
        s, wide = attend(j, chip_slots)
        top = jnp.max(s, axis=1, keepdims=True)
        p = jnp.exp2(s - top).astype(bf16)
        o = dot(p, wide)
        acc[j] = o[:, :AD]
        lsum[j] = o[:, AD:]
        mtop[j] = jnp.broadcast_to(top, (ratio * TOK, AD))

    def fold(j, slots):
        s, wide = attend(j, slots)
        before = mtop[j]
        top = jnp.maximum(before, jnp.max(s, axis=1, keepdims=True))
        p = jnp.exp2(s - jnp.concatenate([top] * len(slots), axis=1)).astype(bf16)
        o = dot(p, wide)
        fade = jnp.exp2(before - top)
        return acc[j] * fade + o[:, :AD], lsum[j] * fade + o[:, AD:], top

    arrived(1)

    @pl.when(odd)
    def _():
        combine(NG - 2)
        combine(NG - 1)

    start(relays[:2])
    arrived(5)
    start(relays[2:])
    @pl.when(even)
    def _():
        arrived(2)

    start(far)

    @pl.when(even)
    def _():
        arrived(6)

    @pl.when(odd)
    def _():
        arrived(4)
        arrived(0)

    def relay_state(g):
        up = remote(abuf.at[g], bbuf.at[g], rel1.at[g], b_recv.at[g], b + 1)
        over = remote(hsend.at[g], hbuf.at[g], h_send.at[g], h_recv.at[g], b + 2)
        return up, over

    def unpack(raw):
        built = dot(raw[HALF:, :N], raw[:HALF, :], TN)
        return jnp.where(rows_in > 0.5, built, raw.astype(f32)).astype(bf16)

    def pass_on(g):
        @pl.when(even & bwd1)
        def _():
            state_copy(g).wait_recv()
            up, over = relay_state(g)

            up.start()

            @pl.when(fwd2)
            def _():
                raw = abuf[g]
                c_rows = chead[:, pl.ds(pl.multiple_of(g * N, N), N)]
                seen = dot(c_rows, raw)
                kept = jnp.where(rows_in > 0.5, raw[:HALF].astype(f32), seen)
                hsend[g, :, :GW] = kept.astype(bf16)
                hsend[g, :, GW:] = raw[HALF:, :N]
                over.start()

            c_grp = c_ref[:, pl.ds(pl.multiple_of(g * N, N), N)]
            raw = abuf[g]
            upper = raw[:HALF].astype(f32)
            brief = jnp.concatenate([upper, jnp.zeros_like(upper)], axis=0)
            got = jnp.where(short_in > 0.5, brief, dot(c_grp, unpack(raw)))
            res[g] = res[g] + got * fx[g]

    @pl.when(even & fwd2)
    def _():
        remote(chead, chead, ch_send, ch_recv, b).wait_recv()

    @pl.loop(0, AK)
    def _(j):
        acc[j], lsum[j], mtop[j] = fold(j, near_slots)

        @pl.when(j % 2 == 1)
        def _():
            pass_on(j // 2)


    @pl.when(even & (b >= REACH))
    def _():
        for copy in half_kv(b):
            copy.wait_recv()
        kbuf[0, :HALF, :] = abuf[NG - 2, HALF:, :]
        vbuf[0, :HALF, :] = abuf[NG - 1, HALF:, :]

    @pl.when(odd)
    def _():
        arrived(6)

    @pl.loop(0, AK)
    def _(j):
        weighted_sum, total, _ = fold(j, far_slots)
        out = (weighted_sum / total).astype(bf16)
        square = jnp.zeros((TOK, AD), f32)
        for r in range(ratio):
            piece = out[r * TOK : (r + 1) * TOK]
            attn_ref[:, pl.ds(pl.multiple_of(j * ratio * AD + r * AD, AD), AD)] = piece
            wide_piece = piece.astype(f32)
            square = square + wide_piece * wide_piece
        esq[1] = esq[1] + square

    @pl.when(even & bwd1)
    def _():
        scale_copy().wait_recv()

    @pl.loop(0, NG)
    def _(g):
        c_grp = c_ref[:, pl.ds(pl.multiple_of(g * N, N), N)]

        @pl.when(even)
        def _():
            @pl.when(b >= 4)
            def _():
                remote(hbuf.at[g], hbuf.at[g], h_send.at[g], h_recv.at[g], b).wait_recv()

            half = hbuf[g, :, :GW]
            built = dot(hbuf[g, :, GW:], half, TN).astype(bf16)
            seen = half.astype(f32)
            seen = jnp.concatenate([seen, jnp.zeros_like(seen)], axis=0)
            far_part = jnp.where(rows_before > 0.5, dot(c_grp, built), seen)
            reach[...] = far_part * sbuf[g]

        @pl.when(odd)
        def _():
            @pl.when(b >= 3)
            def _():
                remote(bbuf.at[g], bbuf.at[g], rel1.at[g], b_recv.at[g], b).wait_recv()

            reach[...] = dot(c_grp, abuf[g]) + dot(c_grp, unpack(bbuf[g])) * sbuf[g]

        reached = reach[...]
        lanes = pl.ds(pl.multiple_of(g * GW, GW), GW)
        result = res[g] + reached * fx[g]
        gated = result * lift[g]
        square = jnp.sum(gated * gated, axis=1, keepdims=True) * (1.0 / GW)
        mixed = (gated * lax.rsqrt(square + norm_eps) * gain_ref[:, lanes]).astype(bf16)
        mamba_ref[:, lanes] = mixed
        again = mixed.astype(f32)
        again = again * again
        part = again[:, :TOK]
        for i in range(1, GW // TOK):
            part = part + again[:, i * TOK : (i + 1) * TOK]
        esq[0] = esq[0] + part

    per_mode = [
        jnp.sum(dot(hot[...], esq[i], NN, HIGHEST), axis=1, keepdims=True) for i in range(2)
    ]
    small = iota((8, TOK), 1)
    denom = float(n_dp * n_ctx * TOK) * float(H * P_SIZE)
    mine = jnp.where(small == 0, per_mode[0], jnp.where(small == 1, per_mode[1], 0.0)) / denom

    def exchange(buf, size, me, base, device_of, value):
        buf[me] = value

        def copy(to_index, from_index):
            return pltpu.make_async_remote_copy(
                src_ref=buf.at[me],
                dst_ref=buf.at[from_index],
                send_sem=en_send.at[base + to_index],
                recv_sem=en_recv.at[base + from_index],
                device_id=device_of(to_index),
                device_id_type=MESH,
            )

        for k in sorted(range(1, size), key=lambda k: -min(k, size - k)):
            copy((me + k) % size, me).start()

        @pl.loop(1, size)
        def _(k):
            other = (me + k) % size
            copy(other, other).wait_recv()

        total = buf[0]
        for i in range(1, size):
            total = total + buf[i]
        return total, lambda k: copy((me + k) % size, me).wait_send()

    done = []
    value = mine
    plans = (
        (e1, near, lane_pos, 0, lambda i: {"ctx": row * near + i}),
        (
            e2,
            n_row * n_dp,
            dp * n_row + row,
            near,
            lambda i: {"dp": i // n_row, "ctx": (i % n_row) * near + lane_pos},
        ),
    )
    for buf, size, me, base, device_of in plans:
        if size > 1:
            value, wait = exchange(buf, size, me, base, device_of, value)
            done.append((size, wait))
    energy_ref[...] = value[:2, :2]

    for size, wait in done:

        @pl.loop(1, size)
        def _(k, wait=wait):
            wait(k)

    sent(sends)
    sent(relays)
    sent(far)

    @pl.when(even | fwd1)
    def _():
        scale_copy().wait_send()

        @pl.loop(0, NG)
        def _(g):
            state_copy(g).wait_send()

    @pl.when(even & bwd2)
    def _():
        near_head_copy().wait_send()
        head_copy().wait_send()

    @pl.when(even & bwd1)
    def _():
        @pl.loop(0, NG)
        def _(g):
            up, over = relay_state(g)
            up.wait_send()

            @pl.when(fwd2)
            def _():
                over.wait_send()


def put_out(*refs):
    sem = refs[-1]
    copies = [pltpu.make_async_copy(refs[i], refs[3 + i], sem.at[i]) for i in range(3)]
    for copy in copies:
        copy.start()
    for copy in copies:
        copy.wait()


def shards(n_dp, n_ctx, near, *args):
    (starts, ends, modes, x, decay, b_in, c_in, gate, skip, gain, q, k, v, lw) = args
    operands = (
        starts,
        ends,
        modes,
        x[0],
        decay[0],
        b_in[0],
        c_in[0],
        gate[0],
        skip,
        gain.reshape(1, H * P_SIZE),
        q[0],
        k[0],
        v[0],
        lw,
    )
    vmem = pl.BlockSpec(memory_space=pltpu.VMEM)
    smem = pl.BlockSpec(memory_space=pltpu.SMEM)
    hbm = pl.BlockSpec(memory_space=pl.ANY)
    specs = [vmem] * 3 + [hbm, vmem, hbm, hbm, hbm, smem, vmem, hbm, hbm, hbm, vmem]
    n_row = n_ctx // near
    V, D = pltpu.VMEM, pltpu.SemaphoreType.DMA
    ratio = AQ // AK
    scratch = [
        V((TOK, H * P_SIZE), bf16),
        V((TOK, NG * N), bf16),
        V((TOK, NG * N), bf16),
        V((TOK, H * P_SIZE), bf16),
        V((TOK, AQ * AD), bf16),
        V((2 * REACH + 1, TOK, AK * AD), bf16),
        V((2 * REACH + 1, TOK, AK * AD), bf16),
        V((NG, N, GW), bf16),
        V((NG, N, GW), bf16),
        V((NG, HALF, GW + N), bf16),
        V((NG, HALF, GW + N), bf16),
        V((HALF, NG * N), bf16),
        V((NG, HALF, GW), bf16),
        V((TOK, GW), f32),
        V((NG, TOK, GW), f32),
        V((NG, 1, GW), f32),
        V((NG, N, GW), bf16),
        V((NG, N, GW), f32),
        V((NG, 1, GW), f32),
        V((NG, 1, GW), f32),
        V((NG, TOK, GW), f32),
        V((NG, TOK, GW), f32),
        V((TOK, WIN), f32),
        V((TOK, TOK), f32),
        V((TOK, TOK), f32),
        V((TOK, TOK), f32),
        V((8, TOK), f32),
        V((NG, TOK, TOK), f32),
        V((H, TOK), f32),
        V((AK, ratio * TOK, AD), f32),
        V((AK, ratio * TOK, AD), f32),
        V((AK, ratio * TOK, AD), f32),
        V((2, TOK, TOK), f32),
        V((near, 8, TOK), f32),
        V((n_row * n_dp, 8, TOK), f32),
        D((7, 2)),
        D((7, 2)),
        D((NG,)),
        D((NG,)),
        D((NG,)),
        D,
        D,
        D((NG,)),
        D((NG,)),
        D((NG,)),
        D,
        D,
        D,
        D((near + n_row * n_dp,)),
        D((near + n_row * n_dp,)),
        D((7,)),
    ]
    mamba, attn, energy = pl.pallas_call(
        functools.partial(body, n_dp, n_ctx, near),
        out_shape=(
            pltpu.VMEM((TOK, H * P_SIZE), bf16),
            pltpu.VMEM((TOK, AQ * AD), bf16),
            pltpu.VMEM((2, 2), f32),
        ),
        in_specs=specs,
        out_specs=(vmem, vmem, vmem),
        scratch_shapes=scratch,
        compiler_params=pltpu.CompilerParams(
            collective_id=0, has_side_effects=True, vmem_limit_bytes=60 * 1024 * 1024
        ),
        name="mixers",
    )(*operands)
    results = (mamba, attn, energy)
    mamba, attn, energy = pl.pallas_call(
        put_out,
        out_shape=tuple(jax.ShapeDtypeStruct(r.shape, r.dtype) for r in results),
        in_specs=[vmem] * 3,
        out_specs=(hbm,) * 3,
        scratch_shapes=[D((3,))],
        name="put_out",
    )(*[pltpu.with_memory_space_constraint(r, pltpu.VMEM) for r in results])
    return mamba[None], attn[None], energy


def solution(mesh):
    placed = (
        P("dp", None),
        P("dp", None),
        P("dp", None),
        P("dp", "ctx", None),
        P("dp", None, "ctx"),
        P("dp", "ctx", None),
        P("dp", "ctx", None),
        P("dp", "ctx", None),
        P(),
        P(),
        P("dp", "ctx", None),
        P("dp", "ctx", None),
        P("dp", "ctx", None),
        P("dp", "ctx"),
    )
    n_dp, n_ctx = mesh.shape["dp"], mesh.shape["ctx"]
    return jax.shard_map(
        functools.partial(shards, n_dp, n_ctx, min(16, n_ctx)),
        mesh=mesh,
        in_specs=placed,
        out_specs=(P("dp", "ctx", None), P("dp", "ctx", None), P()),
        check_vma=False,
    )
```

```python
import functools
import math

import jax
import jax.numpy as jnp
from jax import lax
from jax.experimental import pallas as pl
from jax.experimental.pallas import tpu as pltpu
from jax.sharding import PartitionSpec as P

H = 64
P_SIZE = 64
N = 128
NG = 4
AQ = 32
AK = 8
AD = 128
HALF = 64
REACH = 3
TOK = 128
WIN = (2 * REACH + 1) * TOK
GW = (H // NG) * P_SIZE
HPG = H // NG

norm_eps = 1e-05
masked_score = -1e30
MESH = pl.DeviceIdType.MESH
HIGHEST = lax.Precision.HIGHEST
f32 = jnp.float32
bf16 = jnp.bfloat16
NT = (((1,), (1,)), ((), ()))
TN = (((0,), (0,)), ((), ()))
NN = (((1,), (0,)), ((), ()))


def dot(a, b, dims=NN, precision=None):
    return lax.dot_general(a, b, dims, precision=precision, preferred_element_type=f32)


def iota(shape, axis):
    return lax.broadcasted_iota(jnp.int32, shape, axis)


def body(
    n_dp,
    n_ctx,
    near,
    starts_ref,
    ends_ref,
    modes_ref,
    x_hbm,
    decay_ref,
    b_hbm,
    c_hbm,
    gate_hbm,
    skip_ref,
    gain_ref,
    q_hbm,
    k_hbm,
    v_hbm,
    lw_ref,
    mamba_ref,
    attn_ref,
    energy_ref,
    x_ref,
    b_ref,
    c_ref,
    gate_ref,
    q_ref,
    kbuf,
    vbuf,
    abuf,
    bbuf,
    hbuf,
    hsend,
    chead,
    wtail,
    reach,
    lift,
    sbuf,
    ebuf,
    ewide,
    elow,
    alow,
    tbuf,
    tsend,
    fx,
    res,
    bias,
    mmask,
    lastm,
    carm,
    hot,
    runc,
    runr,
    acc,
    lsum,
    mtop,
    esq,
    e1,
    e2,
    kv_send,
    kv_recv,
    st_send,
    a_recv,
    low_send,
    low_recv,
    b_recv,
    s_send,
    s_recv,
    rel1,
    h_send,
    h_recv,
    ch_send,
    chn_send,
    ch_recv,
    en_send,
    en_recv,
    in_sem,
):
    b = lax.axis_index("ctx")
    dp = lax.axis_index("dp")
    core = b % 2
    row, lane_pos = b // near, b % near
    n_row = n_ctx // near
    seq = n_ctx * TOK
    first = b * TOK
    even, odd = core == 0, core == 1

    def peer(i):
        return {"ctx": i}

    barrier = pltpu.get_barrier_semaphore()

    def greet(device):
        pl.semaphore_signal(barrier, inc=1, device_id=device, device_id_type=MESH)

    columns = n_row * n_dp
    count = near - 1 + columns - 1
    for d in (-2, -1, 1, 2):
        ok = (b + d >= 0) & (b + d < n_ctx)

        @pl.when(ok)
        def _(d=d):
            greet({"ctx": b + d})

        count = count + jnp.where(ok, 1, 0)

    @pl.loop(1, near)
    def _(k):
        greet({"ctx": row * near + (lane_pos + k) % near})

    @pl.loop(1, columns)
    def _(k):
        i = (dp * n_row + row + k) % columns
        greet({"dp": i // n_row, "ctx": (i % n_row) * near + lane_pos})


    loads = [
        pltpu.make_async_copy(src, dst, in_sem.at[i])
        for i, (src, dst) in enumerate(
            (
                (x_hbm, x_ref),
                (b_hbm, b_ref),
                (c_hbm, c_ref),
                (k_hbm, kbuf.at[REACH]),
                (v_hbm, vbuf.at[REACH]),
                (q_hbm, q_ref),
                (gate_hbm, gate_ref),
            )
        )
    ]

    pl.semaphore_wait(barrier, count)

    def remote(src, dst, send, recv, to):
        return pltpu.make_async_remote_copy(
            src_ref=src,
            dst_ref=dst,
            send_sem=send,
            recv_sem=recv,
            device_id=peer(to),
            device_id_type=MESH,
        )

    def kv(which_send, from_slot, to_slot, to):
        k_src = k_hbm if from_slot is None else kbuf.at[from_slot]
        v_src = v_hbm if from_slot is None else vbuf.at[from_slot]
        return (
            remote(k_src, kbuf.at[to_slot], kv_send.at[which_send, 0], kv_recv.at[to_slot, 0], to),
            remote(v_src, vbuf.at[to_slot], kv_send.at[which_send, 1], kv_recv.at[to_slot, 1], to),
        )

    fwd2, bwd2 = b + 2 < n_ctx, b - 2 >= 0
    fwd1, bwd1 = b + 1 < n_ctx, b - 1 >= 0
    has_r2, has_l2 = bwd2, fwd2
    sends = [
        (fwd2, lambda: kv(0, None, 1, b + 2)),
        (bwd2, lambda: kv(1, None, 5, b - 2)),
        (even, lambda: kv(2, None, 2, b + 1)),
        (odd, lambda: kv(2, None, 4, b - 1)),
    ]
    relays = [
        (has_r2 & even, lambda: kv(3, 1, 0, b + 1)),
        (has_r2 & odd, lambda: kv(3, 1, 2, b - 1)),
        (has_l2 & even, lambda: kv(4, 5, 4, b + 1)),
        (has_l2 & odd, lambda: kv(4, 5, 6, b - 1)),
        (has_l2 & even & bwd1, lambda: kv(5, 5, 6, b - 1)),
    ]

    def half_kv(to):
        return tuple(
            remote(buf.at[2, HALF:], buf.at[0, HALF:], kv_send.at[6, i], kv_recv.at[0, i], to)
            for i, buf in enumerate((kbuf, vbuf))
        )

    far = [(even & bwd1 & fwd2, lambda: half_kv(b + 2))]

    def start(plan):
        for when, make in plan:

            @pl.when(when)
            def _(make=make):
                for copy in make():
                    copy.start()

    def sent(plan):
        for when, make in plan:

            @pl.when(when)
            def _(make=make):
                for copy in make():
                    copy.wait_send()

    def arrived(slot):
        @pl.when((b - REACH + slot >= 0) & (b - REACH + slot < n_ctx))
        def _():
            for copy in kv(0, None, slot, b):
                copy.wait_recv()

    start(sends)
    for load in loads:
        load.start()

    def head_copy():
        return remote(c_hbm.at[:HALF], chead, ch_send, ch_recv, b - 2)

    def near_head_copy():
        return remote(c_hbm.at[:HALF], chead, chn_send, ch_recv, b - 1)

    @pl.when(even & bwd2)
    def _():
        near_head_copy().start()
        head_copy().start()

    st_row = starts_ref[...].astype(f32)
    en_row = ends_ref[...].astype(f32)
    mo_row = modes_ref[...].astype(f32)
    docs = st_row.shape[1]
    diag = iota((docs, docs), 0) == iota((docs, docs), 1)

    def column(r):
        return jnp.sum(jnp.where(diag, r, 0.0), axis=1, keepdims=True)

    st_col, en_col, mo_col = column(st_row), column(en_row), column(mo_row)
    first_f = first.astype(f32)
    pos_col = first_f + iota((TOK, 1), 0).astype(f32)
    below = st_row <= pos_col
    member = jnp.where(below & (pos_col < en_row), 1.0, 0.0)
    cnt_col = jnp.sum(jnp.where(below, 1.0, 0.0), axis=1, keepdims=True)
    begin_col = jnp.sum(member * st_row, axis=1, keepdims=True)
    mode_col = jnp.sum(member * mo_row, axis=1, keepdims=True)
    key_pos = first_f - float(REACH * TOK) + iota((1, WIN), 1).astype(f32)
    cnt_row = jnp.sum(jnp.where(st_col <= key_pos, 1.0, 0.0), axis=0, keepdims=True)
    present = (key_pos >= 0.0) & (key_pos < float(seq))
    same = (cnt_row == cnt_col) & present
    allowed = same & ((key_pos <= pos_col) | (mode_col == 1.0))
    bias[...] = jnp.where(allowed, 0.0, masked_score)
    own = slice(REACH * TOK, (REACH + 1) * TOK)
    own_same = cnt_row[:, own] == cnt_col
    mmask[...] = jnp.where(own_same & (iota((TOK, TOK), 1) <= iota((TOK, TOK), 0)), 1.0, 0.0)
    lastm[...] = jnp.broadcast_to(
        jnp.where(cnt_col == cnt_col[TOK - 1 :, :], 1.0, 0.0), (TOK, TOK)
    )
    carried = jnp.where(begin_col < first_f, 1.0, 0.0)
    carm[...] = jnp.broadcast_to(carried, (TOK, TOK))

    def goes_on(base):
        end = jnp.where((st_row < base) & (base <= en_row), en_row, 0.0)
        return jnp.sum(jnp.where(end > base + float(2 * TOK + HALF), 1.0, 0.0), axis=1, keepdims=True)

    def ends_soon(base):
        end = jnp.where((st_row < base) & (base <= en_row), en_row, 0.0)
        return jnp.sum(end, axis=1, keepdims=True) <= base + float(HALF)

    chip_first = (first - core * TOK).astype(f32)
    short_out = jnp.where(ends_soon(first_f + float(TOK)), 1.0, 0.0)
    short_in = jnp.where(ends_soon(chip_first), 1.0, 0.0)
    rows_out = goes_on(first_f + float(TOK))
    rows_in = goes_on(chip_first)
    rows_before = goes_on(chip_first - float(2 * TOK))
    own_pos = key_pos[:, own]
    own_member = jnp.where((st_col <= own_pos) & (own_pos < en_col), 1.0, 0.0)
    mode_row = jnp.sum(own_member * mo_col, axis=0, keepdims=True)
    which = iota((8, TOK), 0).astype(f32)
    hot[...] = jnp.where(which == mode_row, lw_ref[...], 0.0)

    upto = jnp.where(iota((TOK, TOK), 0) >= iota((TOK, TOK), 1), 1.0, 0.0)
    decay = decay_ref[...]
    runr[...] = dot(decay, upto, NT, HIGHEST)
    for g in range(NG):
        runc[g, :, :HPG] = dot(upto, decay[g * HPG : (g + 1) * HPG, :], NT, HIGHEST)
    esq[...] = jnp.zeros_like(esq)

    for i in (0, 1, 2, 4, 5, 6):

        @pl.when((b - REACH + i < 0) | (b - REACH + i >= n_ctx))
        def _(i=i):
            kbuf[i] = jnp.zeros((TOK, AK * AD), bf16)
            vbuf[i] = jnp.zeros((TOK, AK * AD), bf16)

    @pl.when(b == 0)
    def _():
        abuf[...] = jnp.zeros_like(abuf)
        sbuf[...] = jnp.zeros_like(sbuf)

    @pl.when(b < 4)
    def _():
        hbuf[...] = jnp.zeros_like(hbuf)

    @pl.when(b < 3)
    def _():
        bbuf[...] = jnp.zeros_like(bbuf)

    for load in loads[:3]:
        load.wait()

    lane = iota((TOK, TOK), 1)
    left = lane < P_SIZE

    def state_copy(g):
        return remote(ebuf.at[g], abuf.at[g], st_send.at[g], a_recv.at[g], b + 1)

    def low_copy(g):
        return remote(elow.at[g], alow.at[g], low_send.at[g], low_recv.at[g], b + 1)

    def scale_copy():
        return remote(tsend, sbuf, s_send, s_recv, b + 1)

    @pl.loop(0, NG)
    def _(g):
        cols = runc[g]
        parts = []
        for pair in range(HPG // 2):
            at = slice(pair * TOK, (pair + 1) * TOK)
            c0 = jnp.broadcast_to(cols[:, 2 * pair : 2 * pair + 1], (TOK, TOK))
            c1 = jnp.broadcast_to(cols[:, 2 * pair + 1 : 2 * pair + 2], (TOK, TOK))
            both = jnp.where(left, c0, c1)
            end = both[TOK - 1 :, :]
            fx[g, :, at] = jnp.exp(both) * carm[...]
            tbuf[g, :, at] = jnp.exp(end) * carm[TOK - 1 :, :]
            tail = jnp.exp(end - both) * lastm[...]
            lanes = pl.ds(pl.multiple_of(g * GW + pair * TOK, TOK), TOK)
            parts.append((x_ref[:, lanes].astype(f32) * tail).astype(bf16))
        weighted = jnp.concatenate(parts, axis=1)
        wtail[g] = weighted[HALF:, :]
        b_grp = b_ref[:, pl.ds(pl.multiple_of(g * N, N), N)]
        e = dot(b_grp, weighted, TN)
        ewide[g] = e
        ebuf[g] = e.astype(bf16)

        @pl.when(even)
        def _():
            elow[g] = (e - ebuf[g].astype(f32)).astype(bf16)
            state_copy(g).start()
            low_copy(g).start()

    @pl.when(even)
    def _():
        tsend[...] = tbuf[...]
        scale_copy().start()

    @pl.when(odd)
    def _():
        scale_copy().wait_recv()
        tsend[...] = tbuf[...] * sbuf[...]

        @pl.when(fwd1)
        def _():
            scale_copy().start()

    def combine(g):
        state_copy(g).wait_recv()
        low_copy(g).wait_recv()
        state = ewide[g] + tbuf[g] * (abuf[g].astype(f32) + alow[g].astype(f32))
        top = wtail[g].astype(f32)
        b_rows = b_ref[HALF:, g * N : (g + 1) * N].astype(f32)
        low = jnp.concatenate([b_rows, top[:, N:]], axis=1)
        rows = jnp.concatenate([top, low], axis=0)
        kept = jnp.where(rows_out > 0.5, rows, state)
        seen = dot(chead[:, g * N : (g + 1) * N], state.astype(bf16))
        if g == NG - 2:
            low = kbuf[1, :HALF, :].astype(f32)
        if g == NG - 1:
            low = vbuf[1, :HALF, :].astype(f32)
        brief = jnp.concatenate([seen, low], axis=0)
        ebuf[g] = jnp.where(short_out > 0.5, brief, kept).astype(bf16)

        @pl.when(fwd1)
        def _():
            state_copy(g).start()

    @pl.when(odd)
    def _():
        @pl.when(fwd1)
        def _():
            remote(chead, chead, ch_send, ch_recv, b).wait_recv()

        @pl.when(b == n_ctx - 1)
        def _():
            chead[...] = jnp.zeros_like(chead)

        for g in range(NG - 2):
            combine(g)

    for load in loads[3:]:
        load.wait()

    @pl.loop(0, NG)
    def _(g):
        z = gate_ref[:, pl.ds(pl.multiple_of(g * GW, GW), GW)].astype(f32)
        lift[g] = z / (1.0 + jnp.exp(-z))
        lanes_n = pl.ds(pl.multiple_of(g * N, N), N)
        both_docs = dot(c_ref[:, lanes_n], b_ref[:, lanes_n], NT) * mmask[...]
        cols = runc[g]
        rows = runr[pl.ds(pl.multiple_of(g * HPG, HPG), HPG), :]
        for pair in range(HPG // 2):
            at = slice(pair * TOK, (pair + 1) * TOK)
            mixes = []
            for h in (2 * pair, 2 * pair + 1):
                spread = cols[:, h : h + 1] - rows[h : h + 1, :]
                mixes.append((jnp.exp(jnp.minimum(spread, 0.0)) * both_docs).astype(bf16))
            xp = x_ref[:, pl.ds(pl.multiple_of(g * GW + pair * TOK, TOK), TOK)]
            zero = jnp.zeros_like(xp)
            split = jnp.concatenate([jnp.where(left, xp, zero), jnp.where(left, zero, xp)], axis=0)
            inner = dot(jnp.concatenate(mixes, axis=1), split)
            h0 = g * HPG + 2 * pair
            skip = jnp.where(left, skip_ref[h0], skip_ref[h0 + 1])
            res[g, :, at] = inner + skip * xp.astype(f32)


    ratio = AQ // AK
    scale = AD ** (-0.5) * math.log2(math.e)

    def block_lanes(i):
        if isinstance(i, int):
            return slice(i * TOK, (i + 1) * TOK)
        return pl.ds(pl.multiple_of(i * TOK, TOK), TOK)

    def attend(j, slots):
        heads = pl.ds(pl.multiple_of(j * AD, AD), AD)
        q = jnp.concatenate(
            [
                q_ref[:, pl.ds(pl.multiple_of(j * ratio * AD + r * AD, AD), AD)]
                for r in range(ratio)
            ],
            axis=0,
        )
        keys = jnp.concatenate(
            [kbuf[i, :, heads] for i in slots], axis=0
        )
        values = jnp.concatenate(
            [vbuf[i, :, heads] for i in slots], axis=0
        )
        masks = jnp.concatenate([bias[:, block_lanes(i)] for i in slots], axis=1)
        s = dot(q, keys, NT) * scale
        s = s.reshape(ratio, TOK, len(slots) * TOK) + masks[None]
        s = s.reshape(ratio * TOK, len(slots) * TOK)
        wide = jnp.concatenate([values, jnp.ones_like(values)], axis=1)
        return s, wide

    beside = jnp.where(even, REACH + 1, REACH - 1)
    chip_slots = (REACH, beside)
    far_one = jnp.where(even, 0, 2 * REACH)
    near_slots = (1, 5, 2 * REACH - beside, 2 * REACH - far_one)
    far_slots = (far_one,)

    @pl.when(even)
    def _():
        arrived(4)

    @pl.when(odd)
    def _():
        arrived(2)

    @pl.loop(0, AK)
    def _(j):
        s, wide = attend(j, chip_slots)
        top = jnp.max(s, axis=1, keepdims=True)
        p = jnp.exp2(s - top).astype(bf16)
        o = dot(p, wide)
        acc[j] = o[:, :AD]
        lsum[j] = o[:, AD:]
        mtop[j] = jnp.broadcast_to(top, (ratio * TOK, AD))

    def fold(j, slots):
        s, wide = attend(j, slots)
        before = mtop[j]
        top = jnp.maximum(before, jnp.max(s, axis=1, keepdims=True))
        p = jnp.exp2(s - jnp.concatenate([top] * len(slots), axis=1)).astype(bf16)
        o = dot(p, wide)
        fade = jnp.exp2(before - top)
        return acc[j] * fade + o[:, :AD], lsum[j] * fade + o[:, AD:], top

    arrived(1)

    @pl.when(odd)
    def _():
        combine(NG - 2)
        combine(NG - 1)

    start(relays[:2])
    arrived(5)
    start(relays[2:])
    @pl.when(even)
    def _():
        arrived(2)

    start(far)

    @pl.when(even)
    def _():
        arrived(6)

    @pl.when(odd)
    def _():
        arrived(4)
        arrived(0)

    def relay_state(g):
        up = remote(abuf.at[g], bbuf.at[g], rel1.at[g], b_recv.at[g], b + 1)
        over = remote(hsend.at[g], hbuf.at[g], h_send.at[g], h_recv.at[g], b + 2)
        return up, over

    def through_rows(c_grp, b_rows, x_rows):
        return dot(dot(c_grp, b_rows, NT).astype(bf16), x_rows)

    def read_state(c_grp, raw):
        by_rows = through_rows(c_grp, raw[HALF:, :N], raw[:HALF, :])
        return jnp.where(rows_in > 0.5, by_rows, dot(c_grp, raw))

    def pass_on(g):
        @pl.when(even & bwd1)
        def _():
            state_copy(g).wait_recv()
            up, over = relay_state(g)

            up.start()

            @pl.when(fwd2)
            def _():
                raw = abuf[g]
                c_rows = chead[:, pl.ds(pl.multiple_of(g * N, N), N)]
                seen = dot(c_rows, raw)
                kept = jnp.where(rows_in > 0.5, raw[:HALF].astype(f32), seen)
                hsend[g, :, :GW] = kept.astype(bf16)
                hsend[g, :, GW:] = raw[HALF:, :N]
                over.start()

            c_grp = c_ref[:, pl.ds(pl.multiple_of(g * N, N), N)]
            raw = abuf[g]
            upper = raw[:HALF].astype(f32)
            brief = jnp.concatenate([upper, jnp.zeros_like(upper)], axis=0)
            got = jnp.where(short_in > 0.5, brief, read_state(c_grp, raw))
            res[g] = res[g] + got * fx[g]

    @pl.when(even & fwd2)
    def _():
        remote(chead, chead, ch_send, ch_recv, b).wait_recv()

    @pl.loop(0, AK)
    def _(j):
        acc[j], lsum[j], mtop[j] = fold(j, near_slots)

        @pl.when(j % 2 == 1)
        def _():
            pass_on(j // 2)


    @pl.when(even & (b >= REACH))
    def _():
        for copy in half_kv(b):
            copy.wait_recv()
        kbuf[0, :HALF, :] = abuf[NG - 2, HALF:, :]
        vbuf[0, :HALF, :] = abuf[NG - 1, HALF:, :]

    @pl.when(odd)
    def _():
        arrived(6)

    @pl.loop(0, AK)
    def _(j):
        weighted_sum, total, _ = fold(j, far_slots)
        out = (weighted_sum / total).astype(bf16)
        square = jnp.zeros((TOK, AD), f32)
        for r in range(ratio):
            piece = out[r * TOK : (r + 1) * TOK]
            attn_ref[:, pl.ds(pl.multiple_of(j * ratio * AD + r * AD, AD), AD)] = piece
            wide_piece = piece.astype(f32)
            square = square + wide_piece * wide_piece
        esq[1] = esq[1] + square

    @pl.when(even & bwd1)
    def _():
        scale_copy().wait_recv()

    @pl.loop(0, NG)
    def _(g):
        c_grp = c_ref[:, pl.ds(pl.multiple_of(g * N, N), N)]

        @pl.when(even)
        def _():
            @pl.when(b >= 4)
            def _():
                remote(hbuf.at[g], hbuf.at[g], h_send.at[g], h_recv.at[g], b).wait_recv()

            half = hbuf[g, :, :GW]
            seen = half.astype(f32)
            seen = jnp.concatenate([seen, jnp.zeros_like(seen)], axis=0)
            far_part = jnp.where(rows_before > 0.5, through_rows(c_grp, hbuf[g, :, GW:], half), seen)
            reach[...] = far_part * sbuf[g]

        @pl.when(odd)
        def _():
            @pl.when(b >= 3)
            def _():
                remote(bbuf.at[g], bbuf.at[g], rel1.at[g], b_recv.at[g], b).wait_recv()

            reach[...] = (
                dot(c_grp, abuf[g])
                + dot(c_grp, alow[g])
                + read_state(c_grp, bbuf[g]) * sbuf[g]
            )

        reached = reach[...]
        lanes = pl.ds(pl.multiple_of(g * GW, GW), GW)
        result = res[g] + reached * fx[g]
        gated = result * lift[g]
        square = jnp.sum(gated * gated, axis=1, keepdims=True) * (1.0 / GW)
        mixed = (gated * lax.rsqrt(square + norm_eps) * gain_ref[:, lanes]).astype(bf16)
        mamba_ref[:, lanes] = mixed
        again = mixed.astype(f32)
        again = again * again
        part = again[:, :TOK]
        for i in range(1, GW // TOK):
            part = part + again[:, i * TOK : (i + 1) * TOK]
        esq[0] = esq[0] + part

    per_mode = [
        jnp.sum(dot(hot[...], esq[i], NN, HIGHEST), axis=1, keepdims=True) for i in range(2)
    ]
    small = iota((8, TOK), 1)
    denom = float(n_dp * n_ctx * TOK) * float(H * P_SIZE)
    mine = jnp.where(small == 0, per_mode[0], jnp.where(small == 1, per_mode[1], 0.0)) / denom

    def exchange(buf, size, me, base, device_of, value):
        buf[me] = value

        def copy(to_index, from_index):
            return pltpu.make_async_remote_copy(
                src_ref=buf.at[me],
                dst_ref=buf.at[from_index],
                send_sem=en_send.at[base + to_index],
                recv_sem=en_recv.at[base + from_index],
                device_id=device_of(to_index),
                device_id_type=MESH,
            )

        for k in sorted(range(1, size), key=lambda k: -min(k, size - k)):
            copy((me + k) % size, me).start()

        @pl.loop(1, size)
        def _(k):
            other = (me + k) % size
            copy(other, other).wait_recv()

        total = buf[0]
        for i in range(1, size):
            total = total + buf[i]
        return total, lambda k: copy((me + k) % size, me).wait_send()

    done = []
    value = mine
    plans = (
        (e1, near, lane_pos, 0, lambda i: {"ctx": row * near + i}),
        (
            e2,
            n_row * n_dp,
            dp * n_row + row,
            near,
            lambda i: {"dp": i // n_row, "ctx": (i % n_row) * near + lane_pos},
        ),
    )
    for buf, size, me, base, device_of in plans:
        if size > 1:
            value, wait = exchange(buf, size, me, base, device_of, value)
            done.append((size, wait))
    energy_ref[...] = value[:2, :2]

    for size, wait in done:

        @pl.loop(1, size)
        def _(k, wait=wait):
            wait(k)

    sent(sends)
    sent(relays)
    sent(far)

    @pl.when(even | fwd1)
    def _():
        scale_copy().wait_send()

        @pl.loop(0, NG)
        def _(g):
            state_copy(g).wait_send()

    @pl.when(even)
    def _():
        @pl.loop(0, NG)
        def _(g):
            low_copy(g).wait_send()

    @pl.when(even & bwd2)
    def _():
        near_head_copy().wait_send()
        head_copy().wait_send()

    @pl.when(even & bwd1)
    def _():
        @pl.loop(0, NG)
        def _(g):
            up, over = relay_state(g)
            up.wait_send()

            @pl.when(fwd2)
            def _():
                over.wait_send()


def put_out(*refs):
    sem = refs[-1]
    copies = [pltpu.make_async_copy(refs[i], refs[3 + i], sem.at[i]) for i in range(3)]
    for copy in copies:
        copy.start()
    for copy in copies:
        copy.wait()


def shards(n_dp, n_ctx, near, *args):
    (starts, ends, modes, x, decay, b_in, c_in, gate, skip, gain, q, k, v, lw) = args
    operands = (
        starts,
        ends,
        modes,
        x[0],
        decay[0],
        b_in[0],
        c_in[0],
        gate[0],
        skip,
        gain.reshape(1, H * P_SIZE),
        q[0],
        k[0],
        v[0],
        lw,
    )
    vmem = pl.BlockSpec(memory_space=pltpu.VMEM)
    smem = pl.BlockSpec(memory_space=pltpu.SMEM)
    hbm = pl.BlockSpec(memory_space=pl.ANY)
    specs = [vmem] * 3 + [hbm, vmem, hbm, hbm, hbm, smem, vmem, hbm, hbm, hbm, vmem]
    n_row = n_ctx // near
    V, D = pltpu.VMEM, pltpu.SemaphoreType.DMA
    ratio = AQ // AK
    scratch = [
        V((TOK, H * P_SIZE), bf16),
        V((TOK, NG * N), bf16),
        V((TOK, NG * N), bf16),
        V((TOK, H * P_SIZE), bf16),
        V((TOK, AQ * AD), bf16),
        V((2 * REACH + 1, TOK, AK * AD), bf16),
        V((2 * REACH + 1, TOK, AK * AD), bf16),
        V((NG, N, GW), bf16),
        V((NG, N, GW), bf16),
        V((NG, HALF, GW + N), bf16),
        V((NG, HALF, GW + N), bf16),
        V((HALF, NG * N), bf16),
        V((NG, HALF, GW), bf16),
        V((TOK, GW), f32),
        V((NG, TOK, GW), f32),
        V((NG, 1, GW), f32),
        V((NG, N, GW), bf16),
        V((NG, N, GW), f32),
        V((NG, N, GW), bf16),
        V((NG, N, GW), bf16),
        V((NG, 1, GW), f32),
        V((NG, 1, GW), f32),
        V((NG, TOK, GW), f32),
        V((NG, TOK, GW), f32),
        V((TOK, WIN), f32),
        V((TOK, TOK), f32),
        V((TOK, TOK), f32),
        V((TOK, TOK), f32),
        V((8, TOK), f32),
        V((NG, TOK, TOK), f32),
        V((H, TOK), f32),
        V((AK, ratio * TOK, AD), f32),
        V((AK, ratio * TOK, AD), f32),
        V((AK, ratio * TOK, AD), f32),
        V((2, TOK, TOK), f32),
        V((near, 8, TOK), f32),
        V((n_row * n_dp, 8, TOK), f32),
        D((7, 2)),
        D((7, 2)),
        D((NG,)),
        D((NG,)),
        D((NG,)),
        D((NG,)),
        D((NG,)),
        D,
        D,
        D((NG,)),
        D((NG,)),
        D((NG,)),
        D,
        D,
        D,
        D((near + n_row * n_dp,)),
        D((near + n_row * n_dp,)),
        D((7,)),
    ]
    mamba, attn, energy = pl.pallas_call(
        functools.partial(body, n_dp, n_ctx, near),
        out_shape=(
            pltpu.VMEM((TOK, H * P_SIZE), bf16),
            pltpu.VMEM((TOK, AQ * AD), bf16),
            pltpu.VMEM((2, 2), f32),
        ),
        in_specs=specs,
        out_specs=(vmem, vmem, vmem),
        scratch_shapes=scratch,
        compiler_params=pltpu.CompilerParams(
            collective_id=0, has_side_effects=True, vmem_limit_bytes=60 * 1024 * 1024
        ),
        name="mixers",
    )(*operands)
    results = (mamba, attn, energy)
    mamba, attn, energy = pl.pallas_call(
        put_out,
        out_shape=tuple(jax.ShapeDtypeStruct(r.shape, r.dtype) for r in results),
        in_specs=[vmem] * 3,
        out_specs=(hbm,) * 3,
        scratch_shapes=[D((3,))],
        name="put_out",
    )(*[pltpu.with_memory_space_constraint(r, pltpu.VMEM) for r in results])
    return mamba[None], attn[None], energy


def solution(mesh):
    placed = (
        P("dp", None),
        P("dp", None),
        P("dp", None),
        P("dp", "ctx", None),
        P("dp", None, "ctx"),
        P("dp", "ctx", None),
        P("dp", "ctx", None),
        P("dp", "ctx", None),
        P(),
        P(),
        P("dp", "ctx", None),
        P("dp", "ctx", None),
        P("dp", "ctx", None),
        P("dp", "ctx"),
    )
    n_dp, n_ctx = mesh.shape["dp"], mesh.shape["ctx"]
    return jax.shard_map(
        functools.partial(shards, n_dp, n_ctx, min(16, n_ctx)),
        mesh=mesh,
        in_specs=placed,
        out_specs=(P("dp", "ctx", None), P("dp", "ctx", None), P()),
        check_vma=False,
    )
```
